1024 devices in a mesh: comp: 2 (over core), lat: 32 (over x, z_hi), lon: 16 (over z_lo, y).
Axes of the slice: x: 8, y: 8, z: 8 (z_hi: 4, z_lo: 2; z = z_hi * 2 + z_lo), core: 2. Of those that a mesh axis runs over, the one named last changes fastest.
Arguments:
- state: float32 [2, 80, 256, 2048], P('comp', None, 'lat', 'lon')
- mixing: float32 [2, 80, 80], P('comp')
- diffusivity: float32 [2, 80], P('comp'), may hold values from 0.22 to 0.25
- weights: float32 [2, 64], P('comp'), may hold values from 0.25 to 1
- links: int32 [2, 32, 16, 4, 32], P('comp', 'lat', 'lon'), may hold values from 0 to 63, as said below
- land: int32 [256, 16], P('lat', 'lon'), may hold values 0 or 1
- depth: int32 [256, 16], P('lat', 'lon'), may hold values from 79 to 80
Outputs:
- advanced: float32 [2, 80, 256, 2048], P('comp', None, 'lat', 'lon')
The draws below stay inside these ranges and needn't reach their ends.
Inputs may be any that keep to these rules, and one draw needn't show every extreme that they name: Entries are source row below 8, destination lon index below 16, destination row below 8, weight index below 64. A device's links come in 8 consecutive groups of 4, each group with one destination, distinct within the device; in every latitude row of a section, the first group of every device has the same destination.
All inputs are finite; a program needn't handle non-finite values. No bound on the sum of `land` on one device may be relied on, other than what follows from the above.
Results may differ from the reference program's by a relative error of at most 0.0003.
Values sent between devices are 32-bit elements; how exact they have to be, the bound alone decides.
A program may use at most 32 MiB of HBM per device.

```python
import math
import jax
import jax.numpy as jnp
from jax import lax

LEV = 80
ROWS = 8
BLOCK = 128
STEPS = 4
CAP = 4
NWEIGHT = 64
LINK_GROUPS = 8
LINKS = 32
NROW = 256
NCOL = 2048
N_LAT = 32
N_LON = 16


def draw_state(key, part):
    shape = (2, LEV, NROW, NCOL)
    base = jnp.clip(jax.random.normal(key, shape, jnp.float32), -3.5, 3.5)
    along = jnp.roll(base, 2, axis=3) - 2.0 * base + jnp.roll(base, -2, axis=3)
    across = jnp.roll(along, 2, axis=2) - 2.0 * along + jnp.roll(along, -2, axis=2)
    return (across * 0.5).astype(jnp.float32)


def draw_mixing(key, part):
    keys = jax.random.split(key, 2)
    diagonal = jax.random.uniform(keys[0], (2, LEV), jnp.float32, 0.92, 1.0)
    offdiag = jax.random.normal(keys[1], (2, LEV, LEV), jnp.float32) * (0.25 / LEV ** 0.5)
    level_ids = jnp.arange(LEV)
    identity = (level_ids[:, None] == level_ids[None, :]).astype(jnp.float32)
    return (offdiag * (1.0 - identity) + identity * diagonal[:, :, None]).astype(jnp.float32)


def draw_links(key, part):
    keys = jax.random.split(key, 5)
    hottest = jax.random.randint(keys[0], (2, N_LAT, 1, 1), 0, N_LON)
    scores = jax.random.randint(keys[1], (2, N_LAT, N_LON, N_LON), 1, 1000)
    order = jnp.arange(N_LON, dtype=jnp.int32)
    scores = scores * N_LON + order
    scores = jnp.where(order == hottest, 0, scores)
    chosen = jnp.argsort(scores, axis=-1, stable=True)[..., :LINK_GROUPS].astype(jnp.int32)
    targets = jnp.repeat(chosen, CAP, axis=-1)
    sources = jax.random.randint(keys[2], (2, N_LAT, N_LON, LINKS), 0, ROWS)
    dest_rows = jax.random.randint(keys[3], (2, N_LAT, N_LON, LINKS), 0, ROWS)
    weight_ids = jax.random.randint(keys[4], (2, N_LAT, N_LON, LINKS), 0, NWEIGHT)
    return jnp.stack([sources, targets, dest_rows, weight_ids], axis=3).astype(jnp.int32)


def with_ends(drawn, rng, low, top_value):
    index_at = [jax.random.randint(jax.random.fold_in(rng, axis), (), 0, length) for axis, length in enumerate(drawn.shape)]
    longest = drawn.shape.index(max(drawn.shape))
    beside = index_at[:longest] + [(index_at[longest] + 1) % drawn.shape[longest]] + index_at[longest + 1:]
    return drawn.at[tuple(index_at)].set(low).at[tuple(beside)].set(top_value)


def block_scale(stream_key, extent, pieces, smallest, top_value):
    level, own = 1.0, jax.random.fold_in(stream_key, 6)
    for position, parts in pieces:
        steps = jnp.exp(jax.random.uniform(jax.random.fold_in(own, position), (parts,), jnp.float32, smallest / len(pieces), top_value / len(pieces)))
        level = level * jnp.repeat(steps, extent[position] // parts).reshape([-1 if axis == position else 1 for axis in range(len(extent))])
    return level


def setup_inputs(seed: int = 0) -> dict:
    key_list = jax.random.split(jax.random.key(seed), 8)
    state = draw_state(jax.random.fold_in(key_list[7], 71), 0)
    mixing = draw_mixing(jax.random.fold_in(key_list[7], 71), 0)
    diffusivity = jnp.clip(jnp.exp(math.log(0.25) - 0.12783338 * jax.random.uniform(key_list[2], (2, LEV), jnp.float32) ** block_scale(key_list[2], (2, LEV), ((0, 2),), -0.2, 0.2)), 0.22, 0.25)
    weights = jnp.clip(0.25 + 0.75 * jax.random.uniform(key_list[3], (2, NWEIGHT), jnp.float32) ** block_scale(key_list[3], (2, NWEIGHT), ((0, 2),), -0.2, 0.2), 0.25, 1.0)
    links = draw_links(jax.random.fold_in(key_list[7], 71), 0)
    land = with_ends((jax.random.randint(key_list[5], (NROW, N_LON), 0, 64) < 63).astype(jnp.int32), jax.random.fold_in(key_list[5], 1), 0, 1)
    depth = with_ends(jax.random.randint(key_list[6], (NROW, N_LON), LEV - 1, LEV + 1), jax.random.fold_in(key_list[6], 1), LEV - 1, LEV).astype(jnp.int32)
    return dict(state=state, mixing=mixing, diffusivity=diffusivity, weights=weights, links=links, land=land, depth=depth)


coupling_rate = 0.5


def regrid(surface, link_table, table):
    blocks = surface.reshape(N_LAT, ROWS, N_LON, BLOCK)
    sources = link_table[:, :, 0]
    targets = link_table[:, :, 1]
    dest_rows = link_table[:, :, 2]
    weight_ids = link_table[:, :, 3]
    lat_ids = jnp.arange(N_LAT, dtype=jnp.int32)[:, None, None]
    lon_ids = jnp.arange(N_LON, dtype=jnp.int32)[None, :, None]
    weight_link = table[weight_ids]
    values = blocks[lat_ids, sources, lon_ids] * weight_link[..., None]
    accum = jnp.zeros((N_LAT, ROWS, N_LON, BLOCK), jnp.float32).at[lat_ids, dest_rows, targets].add(values)
    totals = jnp.zeros((N_LAT, ROWS, N_LON), jnp.float32).at[lat_ids, dest_rows, targets].add(weight_link)
    return (accum / jnp.maximum(totals, 1.0)[..., None]).reshape(NROW, NCOL)


def reference(state, mixing, diffusivity, weights, links, land, depth):
    sea_cells = jnp.repeat(land.astype(jnp.float32), BLOCK, axis=1)
    deep_cells = jnp.repeat((land * depth).astype(jnp.float32), BLOCK, axis=1)
    surfaces = state[:, 0]
    imported = jnp.stack([regrid(surfaces[1], links[1], weights[1]), regrid(surfaces[0], links[0], weights[0])])
    flux_field = coupling_rate * sea_cells[None] * (imported - surfaces)
    level_ids = jnp.arange(LEV, dtype=jnp.float32)[:, None, None]

    def section(packed):
        tracer, mix_mat, diffuse, flux_one, section_id = packed
        ocean_part = (level_ids < deep_cells[None]).astype(jnp.float32)
        active = jnp.where(section_id == 1, ocean_part, jnp.ones_like(ocean_part))
        for step in range(STEPS):
            padded = jnp.pad(tracer, ((0, 0), (1, 1), (0, 0)))
            neighbours = padded[:, 2:] + padded[:, :-2] + jnp.roll(tracer, -1, axis=2) + jnp.roll(tracer, 1, axis=2)
            moved = tracer + diffuse[:, None, None] * (neighbours - 4.0 * tracer)
            moved = moved.at[0].add(flux_one)
            mixed = jnp.dot(mix_mat, (moved * active).reshape(LEV, -1), precision=lax.Precision.HIGHEST, preferred_element_type=jnp.float32).reshape(tracer.shape)
            tracer = active * mixed + (1.0 - active) * tracer
        return tracer

    return lax.map(section, (state, mixing, diffusivity, flux_field, jnp.arange(2, dtype=jnp.int32)))
```

```python
import functools

import jax
import jax.numpy as jnp
from jax import lax
from jax.experimental import pallas as pl
from jax.experimental.pallas import tpu as pltpu
from jax.sharding import PartitionSpec as P

MESH = pl.DeviceIdType.MESH
STEPS = 4
LEV = 80
ROWS = 8
LANES = 128
LINKS = 32
GROUPS = LEV // 8
EXT = ROWS + 2 * STEPS
SIDE = EXT
RATE = 0.5
F32 = jnp.float32
BF16 = jnp.bfloat16


def split3(value):
    high = value.astype(BF16)
    rest = value - high.astype(F32)
    middle = rest.astype(BF16)
    low = (rest - middle.astype(F32)).astype(BF16)
    return high, middle, low


def exact_dot(onehot, value):
    return sum(jnp.dot(onehot, part, preferred_element_type=F32) for part in split3(value))


def column(row, size):
    eye = lax.broadcasted_iota(jnp.int32, (size, size), 0) == lax.broadcasted_iota(jnp.int32, (size, size), 1)
    return jnp.sum(jnp.where(eye, jnp.broadcast_to(row, (size, size)), 0.0), axis=1, keepdims=True)


def kernel(
    n_lat,
    n_lon,
    state,
    mixing,
    diffusivity,
    weights,
    links,
    land,
    depth,
    out,
    xa,
    xb,
    surf,
    mixbuf,
    difbuf,
    wbuf,
    lkbuf,
    landbuf,
    depthbuf,
    mcat,
    pack,
    west,
    east,
    outgoing,
    incoming,
    corner_up,
    corner_down,
    from_up,
    from_down,
    flux_up,
    flux_down,
    fluxes_up,
    fluxes_down,
    load_sem,
    row_send,
    row_recv,
    side_send,
    side_recv,
    regrid_send,
    regrid_recv,
    corner_send,
    corner_recv,
    flux_send,
    flux_recv,
):
    comp, lat, lon = lax.axis_index("comp"), lax.axis_index("lat"), lax.axis_index("lon")
    other = 1 - comp
    up, down = lax.rem(lat + n_lat - 1, n_lat), lax.rem(lat + 1, n_lat)
    left, right = lax.rem(lon + n_lon - 1, n_lon), lax.rem(lon + 1, n_lon)

    barrier = pltpu.get_barrier_semaphore()
    for device in ({"lat": up}, {"lat": down}, {"lon": left}, {"lon": right}):
        pl.semaphore_signal(barrier, inc=1, device_id=device, device_id_type=MESH)
    for d in range(n_lon):
        pl.semaphore_signal(barrier, inc=1, device_id={"comp": other, "lon": d}, device_id_type=MESH)

    loads = [
        pltpu.make_async_copy(links.at[0, 0, 0], lkbuf, load_sem.at[0]),
        pltpu.make_async_copy(weights, wbuf, load_sem.at[1]),
        pltpu.make_async_copy(state.at[0, 0], surf, load_sem.at[2]),
        pltpu.make_async_copy(land, landbuf, load_sem.at[3]),
        pltpu.make_async_copy(depth, depthbuf, load_sem.at[4]),
        pltpu.make_async_copy(mixing.at[0], mixbuf, load_sem.at[5]),
        pltpu.make_async_copy(diffusivity, difbuf, load_sem.at[6]),
    ]
    for r in range(ROWS):
        loads.append(pltpu.make_async_copy(state.at[0, :, r, :], xa.at[STEPS + r], load_sem.at[7 + r]))
    for load in loads:
        load.start()

    lane = lax.broadcasted_iota(jnp.int32, (1, LANES), 1)
    cell = lane & 7
    low_half = cell < 4
    sub8 = lax.broadcasted_iota(jnp.int32, (8, LANES), 0)
    lane8 = lax.broadcasted_iota(jnp.int32, (8, LANES), 1)

    for load in loads[:3]:
        load.wait()
    table = lkbuf[...].astype(F32)
    source_row, target_row, dest_row, weight_row = (table[i : i + 1, :] for i in range(4))
    source_col, dest_col, weight_col = (column(row, LINKS) for row in (source_row, dest_row, weight_row))
    weight_ids = lax.broadcasted_iota(jnp.int32, (LINKS, wbuf.shape[1]), 1).astype(F32)
    weight = jnp.sum(
        jnp.where(weight_col == weight_ids, jnp.broadcast_to(wbuf[...], weight_ids.shape), 0.0), axis=1, keepdims=True
    )
    surface = surf[...]
    picked = jnp.zeros((LINKS, LANES), F32)
    for b in range(ROWS):
        picked = jnp.where(source_col == float(b), surface[b : b + 1, :], picked)
    row_id = lax.broadcasted_iota(jnp.int32, (n_lon * 8, LINKS), 0)
    place = (row_id.astype(F32) == target_row * 8.0 + dest_row).astype(F32).astype(BF16)
    outgoing[:, 0:8, :] = exact_dot(place, picked * weight).reshape(n_lon, 8, LANES)
    kind = row_id & 7
    dest = row_id >> 3
    before, after = dest - 1, dest + 1
    before = jnp.where(before < 0, n_lon - 1, before)
    after = jnp.where(after >= n_lon, 0, after)
    wanted = jnp.where(kind < 2, before, jnp.where((kind == 4) | (kind == 5), after, dest))
    wanted = jnp.where((kind == 3) | (kind == 7), -1, wanted)
    place_side = (wanted.astype(F32) == target_row).astype(F32).astype(BF16)
    lane32 = lax.broadcasted_iota(jnp.int32, (LINKS, LANES), 1)
    side_row = ((lane32 >> 3) - STEPS).astype(F32)
    side_weight = jnp.where(dest_col == side_row, weight, 0.0)
    ends = jnp.where(lane32 < 8, pltpu.roll(picked, 4, 1), 0.0)
    for shift in (8, 16, 32, 64):
        ends = ends + pltpu.roll(ends, shift, 1)
    both = exact_dot(place_side, jnp.concatenate([side_weight * ends, side_weight], axis=1))
    both = both.reshape(n_lon, 8, 2 * LANES)
    kind3 = lax.broadcasted_iota(jnp.int32, (n_lon, 8, LANES), 1)
    merged = jnp.where((kind3 & 3) == 0, both[:, :, :LANES], both[:, :, LANES:])
    outgoing[:, 8:16, :] = jnp.where(low_half, merged, pltpu.roll(merged, 4, 1))

    loads[3].wait()
    loads[4].wait()
    land_col = landbuf[...].astype(F32)
    depth_col = jnp.where(comp == 1, land_col * depthbuf[...].astype(F32), float(LEV))
    land_own = jnp.broadcast_to(land_col, (8, LANES))
    depth_own = jnp.broadcast_to(depth_col, (8, LANES))
    mine = (lane8 >> 3) == sub8
    depth_ends = jnp.sum(jnp.where(mine, depth_own, 0.0), axis=0, keepdims=True)
    land_ends = jnp.sum(jnp.where(mine, land_own, 0.0), axis=0, keepdims=True)
    pack[5 * 8 :, :] = jnp.where(sub8 == 0, depth_ends, land_ends)

    for load in loads[7:]:
        load.wait()

    def gather_ends(src, rows, offset):
        total = None
        for e in rows:
            rolled = pltpu.roll(src[e], (e * 8 + 4) % LANES, 1)
            total = rolled if total is None else jnp.where((lane >> 3) == e, rolled, total)
        return total

    own_ends = gather_ends(xa, range(STEPS, STEPS + ROWS), 0)
    lower = pltpu.roll(own_ends[: LEV // 2], LANES - 32, 1)
    upper = pltpu.roll(own_ends[LEV // 2 :], 32, 1)
    pack[: LEV // 2, :] = jnp.where(lane < 64, lower, upper)

    pl.semaphore_wait(barrier, 4 + n_lon)

    to_right = pltpu.make_async_remote_copy(
        pack, west, side_send.at[0], side_recv.at[0], device_id={"lon": right}, device_id_type=MESH
    )
    to_left = pltpu.make_async_remote_copy(
        pack, east, side_send.at[1], side_recv.at[1], device_id={"lon": left}, device_id_type=MESH
    )
    to_right.start()
    to_left.start()
    regrids = []
    for k in sorted(range(n_lon), key=lambda k: -min(k % 8, 8 - k % 8)):
        d = lax.rem(lon + k, n_lon)
        copy = pltpu.make_async_remote_copy(
            outgoing.at[d, 0:11],
            incoming.at[lon, 0:11],
            regrid_send.at[k],
            regrid_recv.at[lon],
            device_id={"comp": other, "lon": d},
            device_id_type=MESH,
        )
        copy.start()
        regrids.append(copy)
    rows_out = []
    for ring in range(STEPS):
        rows_out.append(
            pltpu.make_async_remote_copy(
                xa.at[STEPS + ring],
                xa.at[STEPS + ROWS + ring],
                row_send.at[2 * ring],
                row_recv.at[2 * ring],
                device_id={"lat": up},
                device_id_type=MESH,
            )
        )
        rows_out.append(
            pltpu.make_async_remote_copy(
                xa.at[STEPS + ROWS - 1 - ring],
                xa.at[STEPS - 1 - ring],
                row_send.at[2 * ring + 1],
                row_recv.at[2 * ring + 1],
                device_id={"lat": down},
                device_id_type=MESH,
            )
        )
    for copy in rows_out[:4]:
        copy.start()

    loads[5].wait()
    loads[6].wait()
    mix = mixbuf[...]
    mix_high = mix.astype(BF16).astype(F32)
    mcat[:, 0:LEV] = mix_high
    mcat[:, LEV : 2 * LEV] = mix_high
    mcat[:, 2 * LEV : 3 * LEV] = mix - mix_high
    mcat[:, 3 * LEV :] = jnp.zeros((LEV, 16), F32)
    operator = mcat[...].astype(BF16)
    diffuse = jnp.broadcast_to(column(difbuf[...], LEV), (LEV, LANES))
    level = lax.broadcasted_iota(jnp.int32, (LEV, LANES), 0).astype(F32)

    to_right.wait_recv()
    to_left.wait_recv()
    arrived = jnp.where(low_half, west[...], east[...])
    side_own = jnp.concatenate(
        [pltpu.roll(arrived[: LEV // 2], 32, 1), pltpu.roll(arrived[: LEV // 2], LANES - 32, 1)], axis=0
    )
    masks = pltpu.roll(arrived[LEV // 2 :], 32, 1)
    depth_side, land_side = masks[0:1], masks[1:2]

    def corner(target, base):
        for v in range(3):
            groups = range(v * 4, min(v * 4 + 4, GROUPS))
            total = None
            for m, g in enumerate(groups):
                rolled = pltpu.roll(side_own[g * 8 : g * 8 + 8], (m * 32 - base) % LANES, 1)
                total = rolled if total is None else jnp.where((lane >> 5) == m, rolled, total)
            if v == 2:
                total = jnp.where((lane >> 5) == 2, pltpu.roll(jnp.broadcast_to(depth_side, (8, LANES)), (64 - base) % LANES, 1), total)
            target[v * 8 : v * 8 + 8, :] = total
        target[24:32, :] = depth_own

    corner(corner_up, 32)
    corner(corner_down, 64)
    corner_to_up = pltpu.make_async_remote_copy(
        corner_up, from_down, corner_send.at[0], corner_recv.at[0], device_id={"lat": up}, device_id_type=MESH
    )
    corner_to_down = pltpu.make_async_remote_copy(
        corner_down, from_up, corner_send.at[1], corner_recv.at[1], device_id={"lat": down}, device_id_type=MESH
    )
    corner_to_up.start()
    corner_to_down.start()
    for copy in rows_out[4:]:
        copy.start()

    for j in range(n_lon):
        pltpu.make_async_remote_copy(
            outgoing.at[j, 0:11],
            incoming.at[j, 0:11],
            regrid_send.at[j],
            regrid_recv.at[j],
            device_id={"comp": other, "lon": j},
            device_id_type=MESH,
        ).wait_recv()
    accum = incoming[0, 0:8, :]
    extra = incoming[0, 8:11, :]
    for j in range(1, n_lon):
        accum = accum + incoming[j, 0:8, :]
        extra = extra + incoming[j, 8:11, :]
    totals = jnp.sum(
        jnp.where(lane8 == (sub8 + STEPS) * 8, jnp.broadcast_to(extra[2:3], (8, LANES)), 0.0), axis=1, keepdims=True
    )
    flux_own = RATE * land_own * (accum / jnp.maximum(totals, 1.0) - surface)
    flux_side = RATE * land_side * (extra[0:1] / jnp.maximum(extra[1:2], 1.0) - side_own[0:1])
    flux_up[...] = jnp.where(sub8 < 3, flux_own, flux_side)
    flux_down[...] = jnp.where(sub8 >= 5, flux_own, flux_side)
    flux_to_up = pltpu.make_async_remote_copy(
        flux_up, fluxes_down, flux_send.at[0], flux_recv.at[0], device_id={"lat": up}, device_id_type=MESH
    )
    flux_to_down = pltpu.make_async_remote_copy(
        flux_down, fluxes_up, flux_send.at[1], flux_recv.at[1], device_id={"lat": down}, device_id_type=MESH
    )
    flux_to_up.start()
    flux_to_down.start()

    keep_up = jnp.where(lat > 0, 1.0, 0.0)
    keep_down = jnp.where(lat < n_lat - 1, 1.0, 0.0)
    corner_to_up.wait_recv()
    corner_to_down.wait_recv()
    above, below = from_up[...], from_down[...]
    sides = []
    for g in range(GROUPS):
        v, m = divmod(g, 4)
        top = pltpu.roll(above[v * 8 : v * 8 + 8], (0 - m * 32) % LANES, 1) * keep_up
        bottom = pltpu.roll(below[v * 8 : v * 8 + 8], (96 - m * 32) % LANES, 1) * keep_down
        sides.append(jnp.where(lane < 32, top, jnp.where(lane >= 96, bottom, side_own[g * 8 : g * 8 + 8])))
    xa[SIDE] = jnp.concatenate(sides, axis=0)
    depth_top = pltpu.roll(above[16:17], LANES - 64, 1) * keep_up
    depth_bottom = pltpu.roll(below[16:17], 32, 1) * keep_down
    depth_z = jnp.where(lane < 32, depth_top, jnp.where(lane >= 96, depth_bottom, depth_side))
    depths = (
        [above[28 + e : 29 + e] * keep_up for e in range(4)]
        + [depth_own[r : r + 1] for r in range(ROWS)]
        + [below[24 + e : 25 + e] * keep_down for e in range(4)]
        + [depth_z]
    )
    flux_to_up.wait_recv()
    flux_to_down.wait_recv()
    top_flux, bottom_flux = fluxes_up[...], fluxes_down[...]
    flux_z = jnp.where(
        lane < 32,
        pltpu.roll(top_flux[0:1], 64, 1),
        jnp.where(lane >= 96, pltpu.roll(bottom_flux[3:4], 64, 1), flux_side),
    )
    fluxes = (
        [None]
        + [top_flux[5 + e : 6 + e] for e in range(3)]
        + [flux_own[r : r + 1] for r in range(ROWS)]
        + [bottom_flux[e : e + 1] for e in range(3)]
        + [None, flux_z]
    )
    for copy in rows_out:
        copy.wait()

    @pl.when(lat == 0)
    def _():
        xa[0:STEPS] = jnp.zeros((STEPS, LEV, LANES), F32)

    @pl.when(lat == n_lat - 1)
    def _():
        xa[STEPS + ROWS : EXT] = jnp.zeros((STEPS, LEV, LANES), F32)

    first_lane, last_lane = lane == 0, lane == LANES - 1
    pad = jnp.zeros((16, LANES), BF16)

    def operand(centre, neighbours, e):
        moved = centre + diffuse * (neighbours - 4.0 * centre)
        moved = jnp.concatenate([moved[:8] + jnp.where(sub8 == 0, fluxes[e], 0.0), moved[8:]], axis=0)
        active = level < depths[e]
        moved = jnp.where(active, moved, 0.0)
        high = moved.astype(BF16)
        low = (moved - high.astype(F32)).astype(BF16)
        return active, jnp.concatenate([high, low, high, pad], axis=0)

    def side_operand(src, rows):
        z = src[SIDE]
        ends = gather_ends(src, rows, 0)
        from_west = pltpu.roll(jnp.where(cell == 3, ends, z), 1, 1)
        from_east = pltpu.roll(jnp.where(cell == 4, ends, z), LANES - 1, 1)
        neighbours = pltpu.roll(z, 8, 1) + pltpu.roll(z, LANES - 8, 1) + from_west + from_east
        return operand(z, neighbours, SIDE)

    def row_operand(src, e):
        centre = src[e]
        z = pltpu.roll(src[SIDE], (LANES - (e * 8 + 4)) % LANES, 1)
        from_west = pltpu.roll(jnp.where(last_lane, z, centre), 1, 1)
        from_east = pltpu.roll(jnp.where(first_lane, z, centre), LANES - 1, 1)
        return operand(centre, src[e - 1] + src[e + 1] + from_west + from_east, e)

    stores = []
    for step in range(1, STEPS + 1):
        src, dst = (xa, xb) if step % 2 else (xb, xa)
        rows = list(range(step, EXT - step))
        tiles = rows + ([SIDE] if step < STEPS else [])
        for at in range(0, len(tiles), 2):
            pair = tiles[at : at + 2]
            parts = [side_operand(src, rows) if e == SIDE else row_operand(src, e) for e in pair]
            right_side = parts[0][1] if len(pair) == 1 else jnp.concatenate([p[1] for p in parts], axis=1)
            mixed = jnp.dot(operator, right_side, preferred_element_type=F32)
            for i, e in enumerate(pair):
                dst[e] = jnp.where(parts[i][0], mixed[:, i * LANES : (i + 1) * LANES], src[e])
                if step == STEPS:
                    store = pltpu.make_async_copy(
                        dst.at[e], out.at[0, :, e - STEPS, :], load_sem.at[7 + e - STEPS]
                    )
                    store.start()
                    stores.append(store)
    for copy in (to_right, to_left, corner_to_up, corner_to_down, flux_to_up, flux_to_down, *regrids):
        copy.wait_send()
    for store in stores:
        store.wait()


def on_device(n_lat, n_lon, state, mixing, diffusivity, weights, links, land, depth):
    vmem = pltpu.VMEM
    dma = pltpu.SemaphoreType.DMA
    return pl.pallas_call(
        functools.partial(kernel, n_lat, n_lon),
        out_shape=jax.ShapeDtypeStruct(state.shape, F32),
        in_specs=[pl.BlockSpec(memory_space=pl.ANY)] * 7,
        out_specs=pl.BlockSpec(memory_space=pl.ANY),
        scratch_shapes=[
            vmem((EXT + 1, LEV, LANES), F32),
            vmem((EXT + 1, LEV, LANES), F32),
            vmem((8, LANES), F32),
            vmem((LEV, LEV), F32),
            vmem(diffusivity.shape, F32),
            vmem(weights.shape, F32),
            vmem((4, LINKS), jnp.int32),
            vmem(land.shape, jnp.int32),
            vmem(depth.shape, jnp.int32),
            vmem((LEV, 3 * LEV + 16), F32),
            vmem((LEV // 2 + 8, LANES), F32),
            vmem((LEV // 2 + 8, LANES), F32),
            vmem((LEV // 2 + 8, LANES), F32),
            vmem((n_lon, 16, LANES), F32),
            vmem((n_lon, 16, LANES), F32),
            vmem((32, LANES), F32),
            vmem((32, LANES), F32),
            vmem((32, LANES), F32),
            vmem((32, LANES), F32),
            vmem((8, LANES), F32),
            vmem((8, LANES), F32),
            vmem((8, LANES), F32),
            vmem((8, LANES), F32),
            dma((7 + ROWS,)),
            dma((2 * STEPS,)),
            dma((2 * STEPS,)),
            dma((2,)),
            dma((2,)),
            dma((n_lon,)),
            dma((n_lon,)),
            dma((2,)),
            dma((2,)),
            dma((2,)),
            dma((2,)),
        ],
        compiler_params=pltpu.CompilerParams(collective_id=0, has_side_effects=True),
    )(state, mixing, diffusivity, weights, links, land, depth)


def solution(mesh):
    in_specs = (
        P("comp", None, "lat", "lon"),
        P("comp", None, None),
        P("comp", None),
        P("comp", None),
        P("comp", "lat", "lon", None, None),
        P("lat", "lon"),
        P("lat", "lon"),
    )
    return jax.shard_map(
        functools.partial(on_device, mesh.shape["lat"], mesh.shape["lon"]),
        mesh=mesh,
        in_specs=in_specs,
        out_specs=P("comp", None, "lat", "lon"),
        check_vma=False,
    )
```

```python
import functools

import jax
import jax.numpy as jnp
from jax import lax
from jax.experimental import pallas as pl
from jax.experimental.pallas import tpu as pltpu
from jax.sharding import PartitionSpec as P

MESH = pl.DeviceIdType.MESH
STEPS = 4
LEV = 80
ROWS = 8
LANES = 128
LINKS = 32
GROUPS = LEV // 8
EXT = ROWS + 2 * STEPS
SIDE = EXT
RATE = 0.5
F32 = jnp.float32
BF16 = jnp.bfloat16


def split3(value):
    high = value.astype(BF16)
    rest = value - high.astype(F32)
    middle = rest.astype(BF16)
    low = (rest - middle.astype(F32)).astype(BF16)
    return high, middle, low


def ex0ct_dot(onehot, value):
    return sum(jnp.dot(onehot, part, preferred_element_type=F32) for part in split3(value))


def column(row, size):
    eye = lax.broadcasted_iota(jnp.int32, (size, size), 0) == lax.broadcasted_iota(jnp.int32, (size, size), 1)
    return jnp.sum(jnp.where(eye, jnp.broadcast_to(row, (size, size)), 0.0), axis=1, keepdims=True)


def kernel(
    n_lat,
    n_lon,
    state,
    mixing,
    diffusivity,
    weights,
    links,
    land,
    depth,
    out,
    x0,
    x1,
    x2,
    x3,
    x4,
    surf,
    mixbuf,
    difbuf,
    wbuf,
    lkbuf,
    landbuf,
    depthbuf,
    mcat,
    pack,
    west,
    east,
    outgoing,
    incoming,
    corner_up,
    corner_down,
    from_up,
    from_down,
    flux_up,
    flux_down,
    fluxes_up,
    fluxes_down,
    load_sem,
    row_send,
    row_recv,
    side_send,
    side_recv,
    regrid_send,
    regrid_recv,
    corner_send,
    corner_recv,
    flux_send,
    flux_recv,
    handing,
    given,
    hand_send,
    hand_recv,
):
    comp, lat, lon = lax.axis_index("comp"), lax.axis_index("lat"), lax.axis_index("lon")
    other = 1 - comp
    up, down = lax.rem(lat + n_lat - 1, n_lat), lax.rem(lat + 1, n_lat)
    left, right = lax.rem(lon + n_lon - 1, n_lon), lax.rem(lon + 1, n_lon)

    has_up, has_down = lat > 0, lat < n_lat - 1
    barrier = pltpu.get_barrier_semaphore()

    def greet(device):
        pl.semaphore_signal(barrier, inc=1, device_id=device, device_id_type=MESH)

    @pl.when(comp == 1)
    def _():
        for k in range(n_lon):
            greet({"comp": 0, "lon": lax.rem(lon + k, n_lon)})
        for k in range(1, n_lon):
            greet({"lon": lax.rem(lon + k, n_lon)})

    @pl.when(comp == 0)
    def _():
        greet({"comp": 1})
        greet({"lon": left})
        greet({"lon": right})

    @pl.when(has_up)
    def _():
        greet({"lat": up})

    @pl.when(has_down)
    def _():
        greet({"lat": down})

    loads = [
        pltpu.make_async_copy(links.at[0, 0, 0], lkbuf, load_sem.at[0]),
        pltpu.make_async_copy(weights, wbuf, load_sem.at[1]),
        pltpu.make_async_copy(state.at[0, 0], surf, load_sem.at[2]),
        pltpu.make_async_copy(land, landbuf, load_sem.at[3]),
        pltpu.make_async_copy(depth, depthbuf, load_sem.at[4]),
        pltpu.make_async_copy(mixing.at[0], mixbuf, load_sem.at[5]),
        pltpu.make_async_copy(diffusivity, difbuf, load_sem.at[6]),
    ]
    for r in range(ROWS):
        loads.append(pltpu.make_async_copy(state.at[0, :, r, :], x0.at[STEPS + r], load_sem.at[7 + r]))
    for load in loads:
        load.start()

    @pl.when(lat == 0)
    def _():
        x0[0:STEPS] = jnp.zeros((STEPS, LEV, LANES), F32)
        from_up[...] = jnp.zeros((32, LANES), F32)
        fluxes_up[...] = jnp.zeros((8, LANES), F32)

    @pl.when(lat == n_lat - 1)
    def _():
        x0[STEPS + ROWS : EXT] = jnp.zeros((STEPS, LEV, LANES), F32)
        from_down[...] = jnp.zeros((32, LANES), F32)
        fluxes_down[...] = jnp.zeros((8, LANES), F32)

    lane = lax.broadcasted_iota(jnp.int32, (1, LANES), 1)
    cell = lane & 7
    low_half = cell < 4
    sub8 = lax.broadcasted_iota(jnp.int32, (8, LANES), 0)
    lane8 = lax.broadcasted_iota(jnp.int32, (8, LANES), 1)

    for load in loads[:3]:
        load.wait()
    table = lkbuf[...].astype(F32)
    source_row, target_row, dest_row, weight_row = (table[i : i + 1, :] for i in range(4))
    source_col, dest_col, weight_col = (column(row, LINKS) for row in (source_row, dest_row, weight_row))
    weight_ids = lax.broadcasted_iota(jnp.int32, (LINKS, wbuf.shape[1]), 1).astype(F32)
    weight = jnp.sum(
        jnp.where(weight_col == weight_ids, jnp.broadcast_to(wbuf[...], weight_ids.shape), 0.0), axis=1, keepdims=True
    )
    surface = surf[...]
    picked = jnp.zeros((LINKS, LANES), F32)
    for b in range(ROWS):
        picked = jnp.where(source_col == float(b), surface[b : b + 1, :], picked)
    row_id = lax.broadcasted_iota(jnp.int32, (n_lon * 8, LINKS), 0)
    place = (row_id.astype(F32) == target_row * 8.0 + dest_row).astype(F32).astype(BF16)
    outgoing[:, 0:8, :] = ex0ct_dot(place, picked * weight).reshape(n_lon, 8, LANES)
    kind = row_id & 7
    dest = row_id >> 3
    before, after = dest - 1, dest + 1
    before = jnp.where(before < 0, n_lon - 1, before)
    after = jnp.where(after >= n_lon, 0, after)
    wanted = jnp.where(kind < 2, before, jnp.where((kind == 4) | (kind == 5), after, dest))
    wanted = jnp.where((kind == 3) | (kind == 7), -1, wanted)
    place_side = (wanted.astype(F32) == target_row).astype(F32).astype(BF16)
    lane32 = lax.broadcasted_iota(jnp.int32, (LINKS, LANES), 1)
    side_row = ((lane32 >> 3) - STEPS).astype(F32)
    side_weight = jnp.where(dest_col == side_row, weight, 0.0)
    ends = jnp.where(lane32 < 8, pltpu.roll(picked, 4, 1), 0.0)
    for shift in (8, 16, 32, 64):
        ends = ends + pltpu.roll(ends, shift, 1)
    both = ex0ct_dot(place_side, jnp.concatenate([side_weight * ends, side_weight], axis=1))
    both = both.reshape(n_lon, 8, 2 * LANES)
    kind3 = lax.broadcasted_iota(jnp.int32, (n_lon, 8, LANES), 1)
    merged = jnp.where((kind3 & 3) == 0, both[:, :, :LANES], both[:, :, LANES:])
    outgoing[:, 8:16, :] = jnp.where(low_half, merged, pltpu.roll(merged, 4, 1))

    loads[3].wait()
    loads[4].wait()
    land_row = landbuf[...].astype(F32)
    depth_row = jnp.where(comp == 1, land_row * depthbuf[...].astype(F32), float(LEV))
    land_col, depth_col = column(land_row, ROWS), column(depth_row, ROWS)
    land_own = jnp.broadcast_to(land_col, (8, LANES))
    depth_own = jnp.broadcast_to(depth_col, (8, LANES))
    mine = (lane8 >> 3) == sub8
    depth_ends = jnp.sum(jnp.where(mine, depth_own, 0.0), axis=0, keepdims=True)
    land_ends = jnp.sum(jnp.where(mine, land_own, 0.0), axis=0, keepdims=True)
    pack[5 * 8 :, :] = jnp.where(sub8 == 0, depth_ends, land_ends)

    for load in loads[7:]:
        load.wait()

    def gather_ends(src, rows, offset):
        total = None
        for e in rows:
            rolled = pltpu.roll(src[e], (e * 8 + 4) % LANES, 1)
            total = rolled if total is None else jnp.where((lane >> 3) == e, rolled, total)
        return total

    own_ends = gather_ends(x0, range(STEPS, STEPS + ROWS), 0)
    lower = pltpu.roll(own_ends[: LEV // 2], LANES - 32, 1)
    upper = pltpu.roll(own_ends[LEV // 2 :], 32, 1)
    pack[: LEV // 2, :] = jnp.where(lane < 64, lower, upper)

    above_here = 1 - lax.div(n_lat - lat, n_lat)
    below_here = 1 - lax.div(lat + 1, n_lat)
    pl.semaphore_wait(barrier, n_lon + 2 * (1 - comp) + above_here + below_here)

    to_right = pltpu.make_async_remote_copy(
        pack, west, side_send.at[0], side_recv.at[0], device_id={"lon": right}, device_id_type=MESH
    )
    to_left = pltpu.make_async_remote_copy(
        pack, east, side_send.at[1], side_recv.at[1], device_id={"lon": left}, device_id_type=MESH
    )
    to_right.start()
    to_left.start()

    def regrid(k):
        d = lax.rem(lon + k, n_lon)
        return pltpu.make_async_remote_copy(
            outgoing.at[d, 0:11],
            incoming.at[comp, lon, 0:11],
            regrid_send.at[k],
            regrid_recv.at[comp, lon],
            device_id={"comp": 1, "lon": d},
            device_id_type=MESH,
        )

    for k in sorted(range(1, n_lon), key=lambda k: -min(k % 8, 8 - k % 8)):
        regrid(k).start()

    @pl.when(comp == 0)
    def _():
        regrid(0).start()

    kept = pltpu.make_async_copy(outgoing.at[lon, 0:11], incoming.at[1, lon, 0:11], regrid_recv.at[1, lon])

    @pl.when(comp == 1)
    def _():
        kept.start()

    rows_out = []
    for ring in range(STEPS):
        rows_out.append(
            pltpu.make_async_remote_copy(
                x0.at[STEPS + ring],
                x0.at[STEPS + ROWS + ring],
                row_send.at[2 * ring],
                row_recv.at[2 * ring],
                device_id={"lat": up},
                device_id_type=MESH,
            )
        )
        rows_out.append(
            pltpu.make_async_remote_copy(
                x0.at[STEPS + ROWS - 1 - ring],
                x0.at[STEPS - 1 - ring],
                row_send.at[2 * ring + 1],
                row_recv.at[2 * ring + 1],
                device_id={"lat": down},
                device_id_type=MESH,
            )
        )

    def both_ways(act, upward, downward):
        @pl.when(has_up)
        def _():
            for copy in upward:
                act(copy)

        @pl.when(has_down)
        def _():
            for copy in downward:
                act(copy)

    start = lambda copy: copy.start()
    arrive = lambda copy: copy.wait_recv()
    leave = lambda copy: copy.wait_send()
    both_ways(start, rows_out[0:4:2], rows_out[1:4:2])

    loads[5].wait()
    loads[6].wait()
    mix = mixbuf[...]
    mix_high = mix.astype(BF16).astype(F32)
    mcat[:, 0:LEV] = mix_high
    mcat[:, LEV : 2 * LEV] = mix_high
    mcat[:, 2 * LEV : 3 * LEV] = mix - mix_high
    mcat[:, 3 * LEV :] = jnp.zeros((LEV, 16), F32)
    operator = mcat[...].astype(BF16)
    diffuse = jnp.broadcast_to(column(difbuf[...], LEV), (LEV, LANES))
    level = lax.broadcasted_iota(jnp.int32, (LEV, LANES), 0).astype(F32)

    to_right.wait_recv()
    to_left.wait_recv()
    arrived = jnp.where(low_half, west[...], east[...])
    side_own = jnp.concatenate(
        [pltpu.roll(arrived[: LEV // 2], 32, 1), pltpu.roll(arrived[: LEV // 2], LANES - 32, 1)], axis=0
    )
    masks = pltpu.roll(arrived[LEV // 2 :], 32, 1)
    depth_side, land_side = masks[0:1], masks[1:2]

    def corner(target, base):
        for v in range(3):
            groups = range(v * 4, min(v * 4 + 4, GROUPS))
            total = None
            for m, g in enumerate(groups):
                rolled = pltpu.roll(side_own[g * 8 : g * 8 + 8], (m * 32 - base) % LANES, 1)
                total = rolled if total is None else jnp.where((lane >> 5) == m, rolled, total)
            if v == 2:
                total = jnp.where((lane >> 5) == 2, pltpu.roll(jnp.broadcast_to(depth_side, (8, LANES)), (64 - base) % LANES, 1), total)
            target[v * 8 : v * 8 + 8, :] = total
        target[24:32, :] = depth_own

    corner(corner_up, 32)
    corner(corner_down, 64)
    corner_to_up = pltpu.make_async_remote_copy(
        corner_up, from_down, corner_send.at[0], corner_recv.at[0], device_id={"lat": up}, device_id_type=MESH
    )
    corner_to_down = pltpu.make_async_remote_copy(
        corner_down, from_up, corner_send.at[1], corner_recv.at[1], device_id={"lat": down}, device_id_type=MESH
    )
    both_ways(start, [corner_to_up, *rows_out[4::2]], [corner_to_down, *rows_out[5::2]])

    handed = pltpu.make_async_remote_copy(
        handing, given, hand_send, hand_recv, device_id={"comp": 0}, device_id_type=MESH
    )

    def gathered(section):
        for j in range(n_lon):
            copy = pltpu.make_async_remote_copy(
                outgoing.at[j, 0:11],
                incoming.at[section, j, 0:11],
                regrid_send.at[j],
                regrid_recv.at[section, j],
                device_id={"comp": 1, "lon": j},
                device_id_type=MESH,
            )
            copy.wait_recv()
        accum, extra = incoming[section, 0, 0:8, :], incoming[section, 0, 8:11, :]
        for j in range(1, n_lon):
            accum = accum + incoming[section, j, 0:8, :]
            extra = extra + incoming[section, j, 8:11, :]
        return accum, extra

    @pl.when(comp == 1)
    def _():
        accum, extra = gathered(1)
        handing[0:8, :] = accum
        handing[8:11, :] = extra
        handed.start()
        accum, extra = gathered(0)
        given[0:8, :] = accum
        given[8:11, :] = extra

    @pl.when(comp == 0)
    def _():
        handed.wait_recv()

    accum, extra = given[0:8, :], given[8:11, :]
    totals = jnp.sum(
        jnp.where(lane8 == (sub8 + STEPS) * 8, jnp.broadcast_to(extra[2:3], (8, LANES)), 0.0), axis=1, keepdims=True
    )
    flux_own = RATE * land_own * (accum / jnp.maximum(totals, 1.0) - surface)
    flux_side = RATE * land_side * (extra[0:1] / jnp.maximum(extra[1:2], 1.0) - side_own[0:1])
    flux_up[...] = jnp.where(sub8 < 3, flux_own, flux_side)
    flux_down[...] = jnp.where(sub8 >= 5, flux_own, flux_side)
    flux_to_up = pltpu.make_async_remote_copy(
        flux_up, fluxes_down, flux_send.at[0], flux_recv.at[0], device_id={"lat": up}, device_id_type=MESH
    )
    flux_to_down = pltpu.make_async_remote_copy(
        flux_down, fluxes_up, flux_send.at[1], flux_recv.at[1], device_id={"lat": down}, device_id_type=MESH
    )
    both_ways(start, [flux_to_up], [flux_to_down])

    first_lane, last_lane = lane == 0, lane == LANES - 1
    pad = jnp.zeros((16, LANES), BF16)
    levels_at = (x0, x1, x2, x3, x4)
    depths = {STEPS + r: depth_own[r : r + 1] for r in range(ROWS)}
    fluxes = {STEPS + r: flux_own[r : r + 1] for r in range(ROWS)}

    def operand(centre, neighbours, e, step):
        moved = centre + diffuse * (neighbours - 4.0 * centre)
        moved = jnp.concatenate([moved[:8] + jnp.where(sub8 == 0, fluxes[e], 0.0), moved[8:]], axis=0)
        active = level < depths[e]
        moved = jnp.where(active, moved, 0.0)
        high = moved.astype(BF16)
        low = (moved - high.astype(F32)).astype(BF16)
        return active, jnp.concatenate([high, low, high, pad], axis=0)

    def side_operand(src, rows, step):
        z = src[SIDE]
        ends = gather_ends(src, rows, 0)
        from_west = pltpu.roll(jnp.where(cell == 3, ends, z), 1, 1)
        from_east = pltpu.roll(jnp.where(cell == 4, ends, z), LANES - 1, 1)
        neighbours = pltpu.roll(z, 8, 1) + pltpu.roll(z, LANES - 8, 1) + from_west + from_east
        return operand(z, neighbours, SIDE, step)

    def row_operand(src, e, step):
        centre = src[e]
        z = pltpu.roll(src[SIDE], (LANES - (e * 8 + 4)) % LANES, 1)
        from_west = pltpu.roll(jnp.where(last_lane, z, centre), 1, 1)
        from_east = pltpu.roll(jnp.where(first_lane, z, centre), LANES - 1, 1)
        return operand(centre, src[e - 1] + src[e + 1] + from_west + from_east, e, step)

    stores = []

    def advance(step, rows, merge):
        src, dst = levels_at[step - 1], levels_at[step]
        tiles = rows + ([SIDE] if step < STEPS else [])
        for at in range(0, len(tiles), 2):
            pair = tiles[at : at + 2]
            parts = [side_operand(src, rows, step) if e == SIDE else row_operand(src, e, step) for e in pair]
            right_side = parts[0][1] if len(pair) == 1 else jnp.concatenate([p[1] for p in parts], axis=1)
            mixed = jnp.dot(operator, right_side, preferred_element_type=F32)
            for i, e in enumerate(pair):
                new = jnp.where(parts[i][0], mixed[:, i * LANES : (i + 1) * LANES], src[e])
                if e == SIDE and merge:
                    new = jnp.where((lane >> 3) <= rows[-1], new, dst[e])
                if step == STEPS:
                    r = e - STEPS
                    dst[r] = new
                    store = pltpu.make_async_copy(dst.at[r], out.at[0, :, r, :], load_sem.at[7 + r])
                    store.start()
                    stores.append(store)
                else:
                    dst[e] = new

    both_ways(arrive, [], [corner_to_up])
    below = from_down[...]
    sides = []
    for g in range(GROUPS):
        v, m = divmod(g, 4)
        bottom = pltpu.roll(below[v * 8 : v * 8 + 8], (96 - m * 32) % LANES, 1)
        sides.append(jnp.where(lane >= 96, bottom, side_own[g * 8 : g * 8 + 8]))
    x0[SIDE] = jnp.concatenate(sides, axis=0)
    depth_part = jnp.where(lane >= 96, pltpu.roll(below[16:17], 32, 1), depth_side)
    depths.update({STEPS + ROWS + e: below[24 + e : 25 + e] for e in range(4)})
    depths[SIDE] = depth_part
    both_ways(arrive, [], [flux_to_up])
    bottom_flux = fluxes_down[...]
    flux_part = jnp.where(lane >= 96, pltpu.roll(bottom_flux[3:4], 64, 1), flux_side)
    fluxes.update({STEPS + ROWS + e: bottom_flux[e : e + 1] for e in range(3)})
    fluxes[SIDE] = flux_part
    both_ways(arrive, [], rows_out[0::2])
    for step in range(1, STEPS + 1):
        advance(step, list(range(STEPS + step, EXT - step)), False)

    both_ways(arrive, [corner_to_down], [])
    above = from_up[...]
    sides = []
    for g in range(GROUPS):
        v, m = divmod(g, 4)
        top = pltpu.roll(above[v * 8 : v * 8 + 8], (0 - m * 32) % LANES, 1)
        sides.append(jnp.where(lane < 32, top, x0[SIDE, g * 8 : g * 8 + 8]))
    x0[SIDE] = jnp.concatenate(sides, axis=0)
    depths[SIDE] = jnp.where(lane < 32, pltpu.roll(above[16:17], LANES - 64, 1), depth_part)
    depths.update({e: above[28 + e : 29 + e] for e in range(4)})
    both_ways(arrive, [flux_to_down], [])
    top_flux = fluxes_up[...]
    fluxes[SIDE] = jnp.where(lane < 32, pltpu.roll(top_flux[0:1], 64, 1), flux_part)
    fluxes.update({1 + e: top_flux[5 + e : 6 + e] for e in range(3)})
    both_ways(arrive, rows_out[1:4:2], [])
    for step in range(1, STEPS + 1):
        advance(step, [step + 2, step + 3], True)
    both_ways(arrive, rows_out[5::2], [])
    for step in range(1, STEPS + 1):
        advance(step, [step, step + 1], True)
    both_ways(leave, rows_out[0::2], rows_out[1::2])
    for copy in (to_right, to_left, *[regrid(k) for k in range(1, n_lon)]):
        copy.wait_send()

    @pl.when(comp == 0)
    def _():
        regrid(0).wait_send()

    @pl.when(comp == 1)
    def _():
        handed.wait_send()

    both_ways(leave, [corner_to_up, flux_to_up], [corner_to_down, flux_to_down])
    for store in stores:
        store.wait()


def on_device(n_lat, n_lon, state, mixing, diffusivity, weights, links, land, depth):
    vmem = pltpu.VMEM
    dma = pltpu.SemaphoreType.DMA
    return pl.pallas_call(
        functools.partial(kernel, n_lat, n_lon),
        out_shape=jax.ShapeDtypeStruct(state.shape, F32),
        in_specs=[pl.BlockSpec(memory_space=pl.ANY)] * 7,
        out_specs=pl.BlockSpec(memory_space=pl.ANY),
        scratch_shapes=[
            vmem((EXT + 1, LEV, LANES), F32),
            vmem((EXT + 1, LEV, LANES), F32),
            vmem((EXT + 1, LEV, LANES), F32),
            vmem((EXT + 1, LEV, LANES), F32),
            vmem((ROWS, LEV, LANES), F32),
            vmem((8, LANES), F32),
            vmem((LEV, LEV), F32),
            vmem(diffusivity.shape, F32),
            vmem(weights.shape, F32),
            vmem((4, LINKS), jnp.int32),
            vmem((1, ROWS), jnp.int32),
            vmem((1, ROWS), jnp.int32),
            vmem((LEV, 3 * LEV + 16), F32),
            vmem((LEV // 2 + 8, LANES), F32),
            vmem((LEV // 2 + 8, LANES), F32),
            vmem((LEV // 2 + 8, LANES), F32),
            vmem((n_lon, 16, LANES), F32),
            vmem((2, n_lon, 16, LANES), F32),
            vmem((32, LANES), F32),
            vmem((32, LANES), F32),
            vmem((32, LANES), F32),
            vmem((32, LANES), F32),
            vmem((8, LANES), F32),
            vmem((8, LANES), F32),
            vmem((8, LANES), F32),
            vmem((8, LANES), F32),
            dma((7 + ROWS,)),
            dma((2 * STEPS,)),
            dma((2 * STEPS,)),
            dma((2,)),
            dma((2,)),
            dma((n_lon,)),
            dma((2, n_lon)),
            dma((2,)),
            dma((2,)),
            dma((2,)),
            dma((2,)),
            vmem((11, LANES), F32),
            vmem((11, LANES), F32),
            dma,
            dma,
        ],
        compiler_params=pltpu.CompilerParams(collective_id=0, has_side_effects=True),
    )(state, mixing, diffusivity, weights, links, land.reshape(1, ROWS), depth.reshape(1, ROWS))


def solution(mesh):
    in_specs = (
        P("comp", None, "lat", "lon"),
        P("comp", None, None),
        P("comp", None),
        P("comp", None),
        P("comp", "lat", "lon", None, None),
        P("lat", "lon"),
        P("lat", "lon"),
    )
    return jax.shard_map(
        functools.partial(on_device, mesh.shape["lat"], mesh.shape["lon"]),
        mesh=mesh,
        in_specs=in_specs,
        out_specs=P("comp", None, "lat", "lon"),
        check_vma=False,
    )
```

```python
import functools

import jax
import jax.numpy as jnp
from jax import lax
from jax.experimental import pallas as pl
from jax.experimental.pallas import tpu as pltpu
from jax.sharding import PartitionSpec as P

MESH = pl.DeviceIdType.MESH
STEPS = 4
LEV = 80
ROWS = 8
LANES = 128
LINKS = 32
GROUPS = LEV // 8
EXT = ROWS + 2 * STEPS
SIDE = EXT
RATE = 0.5
F32 = jnp.float32
BF16 = jnp.bfloat16


def split3(value):
    high = value.astype(BF16)
    rest = value - high.astype(F32)
    middle = rest.astype(BF16)
    low = (rest - middle.astype(F32)).astype(BF16)
    return high, middle, low


def ex0ct_dot(onehot, value):
    return sum(jnp.dot(onehot, part, preferred_element_type=F32) for part in split3(value))


def column(row, size):
    eye = lax.broadcasted_iota(jnp.int32, (size, size), 0) == lax.broadcasted_iota(jnp.int32, (size, size), 1)
    return jnp.sum(jnp.where(eye, jnp.broadcast_to(row, (size, size)), 0.0), axis=1, keepdims=True)


def kernel(
    n_lat,
    n_lon,
    state,
    mixing,
    diffusivity,
    weights,
    links,
    land,
    depth,
    out,
    x0,
    x1,
    x2,
    x3,
    surf,
    mixbuf,
    difbuf,
    wbuf,
    lkbuf,
    landbuf,
    depthbuf,
    mcat,
    pack,
    west,
    east,
    outgoing,
    incoming,
    corner_up,
    corner_down,
    from_up,
    from_down,
    flux_up,
    flux_down,
    fluxes_up,
    fluxes_down,
    load_sem,
    row_send,
    row_recv,
    side_send,
    side_recv,
    regrid_send,
    regrid_recv,
    corner_send,
    corner_recv,
    flux_send,
    flux_recv,
    handing,
    given,
    hand_send,
    hand_recv,
):
    comp, lat, lon = lax.axis_index("comp"), lax.axis_index("lat"), lax.axis_index("lon")
    other = 1 - comp
    up, down = lax.rem(lat + n_lat - 1, n_lat), lax.rem(lat + 1, n_lat)
    left, right = lax.rem(lon + n_lon - 1, n_lon), lax.rem(lon + 1, n_lon)

    has_up, has_down = lat > 0, lat < n_lat - 1
    barrier = pltpu.get_barrier_semaphore()

    def greet(device):
        pl.semaphore_signal(barrier, inc=1, device_id=device, device_id_type=MESH)

    @pl.when(comp == 1)
    def _():
        for k in range(n_lon):
            greet({"comp": 0, "lon": lax.rem(lon + k, n_lon)})
        for k in range(1, n_lon):
            greet({"lon": lax.rem(lon + k, n_lon)})

    @pl.when(comp == 0)
    def _():
        greet({"comp": 1})
        greet({"lon": left})
        greet({"lon": right})

    @pl.when(has_up)
    def _():
        greet({"lat": up})

    @pl.when(has_down)
    def _():
        greet({"lat": down})

    loads = [
        pltpu.make_async_copy(links.at[0, 0, 0], lkbuf, load_sem.at[0]),
        pltpu.make_async_copy(weights, wbuf, load_sem.at[1]),
        pltpu.make_async_copy(state.at[0, 0], surf, load_sem.at[2]),
        pltpu.make_async_copy(land, landbuf, load_sem.at[3]),
        pltpu.make_async_copy(depth, depthbuf, load_sem.at[4]),
        pltpu.make_async_copy(mixing.at[0], mixbuf, load_sem.at[5]),
        pltpu.make_async_copy(diffusivity, difbuf, load_sem.at[6]),
    ]
    for r in range(ROWS):
        loads.append(pltpu.make_async_copy(state.at[0, :, r, :], x0.at[STEPS + r], load_sem.at[7 + r]))
    for load in loads:
        load.start()

    @pl.when(lat == 0)
    def _():
        x0[0:STEPS] = jnp.zeros((STEPS, LEV, LANES), F32)
        from_up[...] = jnp.zeros((32, LANES), F32)
        fluxes_up[...] = jnp.zeros((8, LANES), F32)

    @pl.when(lat == n_lat - 1)
    def _():
        x0[STEPS + ROWS : EXT] = jnp.zeros((STEPS, LEV, LANES), F32)
        from_down[...] = jnp.zeros((32, LANES), F32)
        fluxes_down[...] = jnp.zeros((8, LANES), F32)

    lane = lax.broadcasted_iota(jnp.int32, (1, LANES), 1)
    cell = lane & 7
    low_half = cell < 4
    sub8 = lax.broadcasted_iota(jnp.int32, (8, LANES), 0)
    lane8 = lax.broadcasted_iota(jnp.int32, (8, LANES), 1)

    for load in loads[:3]:
        load.wait()
    table = lkbuf[...].astype(F32)
    source_row, target_row, dest_row, weight_row = (table[i : i + 1, :] for i in range(4))
    source_col, dest_col, weight_col = (column(row, LINKS) for row in (source_row, dest_row, weight_row))
    weight_ids = lax.broadcasted_iota(jnp.int32, (LINKS, wbuf.shape[1]), 1).astype(F32)
    weight = jnp.sum(
        jnp.where(weight_col == weight_ids, jnp.broadcast_to(wbuf[...], weight_ids.shape), 0.0), axis=1, keepdims=True
    )
    surface = surf[...]
    picked = jnp.zeros((LINKS, LANES), F32)
    for b in range(ROWS):
        picked = jnp.where(source_col == float(b), surface[b : b + 1, :], picked)
    row_id = lax.broadcasted_iota(jnp.int32, (n_lon * 8, LINKS), 0)
    place = (row_id.astype(F32) == target_row * 8.0 + dest_row).astype(F32).astype(BF16)
    outgoing[:, 0:8, :] = ex0ct_dot(place, picked * weight).reshape(n_lon, 8, LANES)
    kind = row_id & 7
    dest = row_id >> 3
    before, after = dest - 1, dest + 1
    before = jnp.where(before < 0, n_lon - 1, before)
    after = jnp.where(after >= n_lon, 0, after)
    wanted = jnp.where(kind < 2, before, jnp.where((kind == 4) | (kind == 5), after, dest))
    wanted = jnp.where((kind == 3) | (kind == 7), -1, wanted)
    place_side = (wanted.astype(F32) == target_row).astype(F32).astype(BF16)
    lane32 = lax.broadcasted_iota(jnp.int32, (LINKS, LANES), 1)
    side_row = ((lane32 >> 3) - STEPS).astype(F32)
    side_weight = jnp.where(dest_col == side_row, weight, 0.0)
    ends = jnp.where(lane32 < 8, pltpu.roll(picked, 4, 1), 0.0)
    for shift in (8, 16, 32, 64):
        ends = ends + pltpu.roll(ends, shift, 1)
    both = ex0ct_dot(place_side, jnp.concatenate([side_weight * ends, side_weight], axis=1))
    both = both.reshape(n_lon, 8, 2 * LANES)
    kind3 = lax.broadcasted_iota(jnp.int32, (n_lon, 8, LANES), 1)
    merged = jnp.where((kind3 & 3) == 0, both[:, :, :LANES], both[:, :, LANES:])
    outgoing[:, 8:16, :] = jnp.where(low_half, merged, pltpu.roll(merged, 4, 1))

    loads[3].wait()
    loads[4].wait()
    land_row = landbuf[...].astype(F32)
    depth_row = jnp.where(comp == 1, land_row * depthbuf[...].astype(F32), float(LEV))
    land_col, depth_col = column(land_row, ROWS), column(depth_row, ROWS)
    land_own = jnp.broadcast_to(land_col, (8, LANES))
    depth_own = jnp.broadcast_to(depth_col, (8, LANES))
    mine = (lane8 >> 3) == sub8
    depth_ends = jnp.sum(jnp.where(mine, depth_own, 0.0), axis=0, keepdims=True)
    land_ends = jnp.sum(jnp.where(mine, land_own, 0.0), axis=0, keepdims=True)
    pack[5 * 8 :, :] = jnp.where(sub8 == 0, depth_ends, land_ends)

    for load in loads[7:]:
        load.wait()

    def gather_ends(src, rows, offset):
        total = None
        for e in rows:
            rolled = pltpu.roll(src[e], (e * 8 + 4) % LANES, 1)
            total = rolled if total is None else jnp.where((lane >> 3) == e, rolled, total)
        return total

    own_ends = gather_ends(x0, range(STEPS, STEPS + ROWS), 0)
    lower = pltpu.roll(own_ends[: LEV // 2], LANES - 32, 1)
    upper = pltpu.roll(own_ends[LEV // 2 :], 32, 1)
    pack[: LEV // 2, :] = jnp.where(lane < 64, lower, upper)

    above_here = 1 - lax.div(n_lat - lat, n_lat)
    below_here = 1 - lax.div(lat + 1, n_lat)
    pl.semaphore_wait(barrier, n_lon + 2 * (1 - comp) + above_here + below_here)

    to_right = pltpu.make_async_remote_copy(
        pack, west, side_send.at[0], side_recv.at[0], device_id={"lon": right}, device_id_type=MESH
    )
    to_left = pltpu.make_async_remote_copy(
        pack, east, side_send.at[1], side_recv.at[1], device_id={"lon": left}, device_id_type=MESH
    )
    to_right.start()
    to_left.start()

    def regrid(k):
        d = lax.rem(lon + k, n_lon)
        return pltpu.make_async_remote_copy(
            outgoing.at[d, 0:11],
            incoming.at[comp, lon, 0:11],
            regrid_send.at[k],
            regrid_recv.at[comp, lon],
            device_id={"comp": 1, "lon": d},
            device_id_type=MESH,
        )

    for k in sorted(range(1, n_lon), key=lambda k: -min(k % 8, 8 - k % 8)):
        regrid(k).start()

    @pl.when(comp == 0)
    def _():
        regrid(0).start()

    kept = pltpu.make_async_copy(outgoing.at[lon, 0:11], incoming.at[1, lon, 0:11], regrid_recv.at[1, lon])

    @pl.when(comp == 1)
    def _():
        kept.start()

    rows_out = []
    for ring in range(STEPS):
        rows_out.append(
            pltpu.make_async_remote_copy(
                x0.at[STEPS + ring],
                x0.at[STEPS + ROWS + ring],
                row_send.at[2 * ring],
                row_recv.at[2 * ring],
                device_id={"lat": up},
                device_id_type=MESH,
            )
        )
        rows_out.append(
            pltpu.make_async_remote_copy(
                x0.at[STEPS + ROWS - 1 - ring],
                x0.at[STEPS - 1 - ring],
                row_send.at[2 * ring + 1],
                row_recv.at[2 * ring + 1],
                device_id={"lat": down},
                device_id_type=MESH,
            )
        )

    def both_ways(act, upward, downward):
        @pl.when(has_up)
        def _():
            for copy in upward:
                act(copy)

        @pl.when(has_down)
        def _():
            for copy in downward:
                act(copy)

    start = lambda copy: copy.start()
    arrive = lambda copy: copy.wait_recv()
    leave = lambda copy: copy.wait_send()
    both_ways(start, rows_out[0:4:2], rows_out[1:4:2])

    loads[5].wait()
    loads[6].wait()
    mix = mixbuf[...]
    mix_high = mix.astype(BF16).astype(F32)
    mcat[:, 0:LEV] = mix_high
    mcat[:, LEV : 2 * LEV] = mix_high
    mcat[:, 2 * LEV : 3 * LEV] = mix - mix_high
    mcat[:, 3 * LEV :] = jnp.zeros((LEV, 16), F32)
    operator = mcat[...].astype(BF16)
    diffuse = jnp.broadcast_to(column(difbuf[...], LEV), (LEV, LANES))
    level = lax.broadcasted_iota(jnp.int32, (LEV, LANES), 0).astype(F32)

    to_right.wait_recv()
    to_left.wait_recv()
    arrived = jnp.where(low_half, west[...], east[...])
    side_own = jnp.concatenate(
        [pltpu.roll(arrived[: LEV // 2], 32, 1), pltpu.roll(arrived[: LEV // 2], LANES - 32, 1)], axis=0
    )
    masks = pltpu.roll(arrived[LEV // 2 :], 32, 1)
    depth_side, land_side = masks[0:1], masks[1:2]

    def corner(target, base):
        for v in range(3):
            groups = range(v * 4, min(v * 4 + 4, GROUPS))
            total = None
            for m, g in enumerate(groups):
                rolled = pltpu.roll(side_own[g * 8 : g * 8 + 8], (m * 32 - base) % LANES, 1)
                total = rolled if total is None else jnp.where((lane >> 5) == m, rolled, total)
            if v == 2:
                total = jnp.where((lane >> 5) == 2, pltpu.roll(jnp.broadcast_to(depth_side, (8, LANES)), (64 - base) % LANES, 1), total)
            target[v * 8 : v * 8 + 8, :] = total
        target[24:32, :] = depth_own

    corner(corner_up, 32)
    corner(corner_down, 64)
    corner_to_up = pltpu.make_async_remote_copy(
        corner_up, from_down, corner_send.at[0], corner_recv.at[0], device_id={"lat": up}, device_id_type=MESH
    )
    corner_to_down = pltpu.make_async_remote_copy(
        corner_down, from_up, corner_send.at[1], corner_recv.at[1], device_id={"lat": down}, device_id_type=MESH
    )
    both_ways(start, [corner_to_up, *rows_out[4::2]], [corner_to_down, *rows_out[5::2]])

    handed = pltpu.make_async_remote_copy(
        handing, given, hand_send, hand_recv, device_id={"comp": 0}, device_id_type=MESH
    )

    def gathered(section):
        for j in range(n_lon):
            copy = pltpu.make_async_remote_copy(
                outgoing.at[j, 0:11],
                incoming.at[section, j, 0:11],
                regrid_send.at[j],
                regrid_recv.at[section, j],
                device_id={"comp": 1, "lon": j},
                device_id_type=MESH,
            )
            copy.wait_recv()
        accum, extra = incoming[section, 0, 0:8, :], incoming[section, 0, 8:11, :]
        for j in range(1, n_lon):
            accum = accum + incoming[section, j, 0:8, :]
            extra = extra + incoming[section, j, 8:11, :]
        return accum, extra

    @pl.when(comp == 1)
    def _():
        accum, extra = gathered(1)
        handing[0:8, :] = accum
        handing[8:11, :] = extra
        handed.start()
        accum, extra = gathered(0)
        given[0:8, :] = accum
        given[8:11, :] = extra

    @pl.when(comp == 0)
    def _():
        handed.wait_recv()

    accum, extra = given[0:8, :], given[8:11, :]
    totals = jnp.sum(
        jnp.where(lane8 == (sub8 + STEPS) * 8, jnp.broadcast_to(extra[2:3], (8, LANES)), 0.0), axis=1, keepdims=True
    )
    flux_own = RATE * land_own * (accum / jnp.maximum(totals, 1.0) - surface)
    flux_side = RATE * land_side * (extra[0:1] / jnp.maximum(extra[1:2], 1.0) - side_own[0:1])
    flux_up[...] = jnp.where(sub8 < 3, flux_own, flux_side)
    flux_down[...] = jnp.where(sub8 >= 5, flux_own, flux_side)
    flux_to_up = pltpu.make_async_remote_copy(
        flux_up, fluxes_down, flux_send.at[0], flux_recv.at[0], device_id={"lat": up}, device_id_type=MESH
    )
    flux_to_down = pltpu.make_async_remote_copy(
        flux_down, fluxes_up, flux_send.at[1], flux_recv.at[1], device_id={"lat": down}, device_id_type=MESH
    )
    both_ways(start, [flux_to_up], [flux_to_down])

    first_lane, last_lane = lane == 0, lane == LANES - 1
    pad = jnp.zeros((16, LANES), BF16)
    levels_at = (x0, x1, x2, x3, out)
    depths = {STEPS + r: depth_own[r : r + 1] for r in range(ROWS)}
    fluxes = {STEPS + r: flux_own[r : r + 1] for r in range(ROWS)}

    def operand(centre, neighbours, e, step):
        moved = centre + diffuse * (neighbours - 4.0 * centre)
        moved = jnp.concatenate([moved[:8] + jnp.where(sub8 == 0, fluxes[e], 0.0), moved[8:]], axis=0)
        active = level < depths[e]
        moved = jnp.where(active, moved, 0.0)
        high = moved.astype(BF16)
        low = (moved - high.astype(F32)).astype(BF16)
        return active, jnp.concatenate([high, low, high, pad], axis=0)

    def side_operand(src, rows, step):
        z = src[SIDE]
        ends = gather_ends(src, rows, 0)
        from_west = pltpu.roll(jnp.where(cell == 3, ends, z), 1, 1)
        from_east = pltpu.roll(jnp.where(cell == 4, ends, z), LANES - 1, 1)
        neighbours = pltpu.roll(z, 8, 1) + pltpu.roll(z, LANES - 8, 1) + from_west + from_east
        return operand(z, neighbours, SIDE, step)

    def row_operand(src, e, step):
        centre = src[e]
        z = pltpu.roll(src[SIDE], (LANES - (e * 8 + 4)) % LANES, 1)
        from_west = pltpu.roll(jnp.where(last_lane, z, centre), 1, 1)
        from_east = pltpu.roll(jnp.where(first_lane, z, centre), LANES - 1, 1)
        return operand(centre, src[e - 1] + src[e + 1] + from_west + from_east, e, step)

    def advance(step, rows, merge):
        src, dst = levels_at[step - 1], levels_at[step]
        tiles = rows + ([SIDE] if step < STEPS else [])
        for at in range(0, len(tiles), 2):
            pair = tiles[at : at + 2]
            parts = [side_operand(src, rows, step) if e == SIDE else row_operand(src, e, step) for e in pair]
            right_side = parts[0][1] if len(pair) == 1 else jnp.concatenate([p[1] for p in parts], axis=1)
            mixed = jnp.dot(operator, right_side, preferred_element_type=F32)
            for i, e in enumerate(pair):
                new = jnp.where(parts[i][0], mixed[:, i * LANES : (i + 1) * LANES], src[e])
                if e == SIDE and merge:
                    new = jnp.where((lane >> 3) <= rows[-1], new, dst[e])
                if step == STEPS:
                    r = e - STEPS
                    dst[r] = new
                else:
                    dst[e] = new

    both_ways(arrive, [], [corner_to_up])
    below = from_down[...]
    sides = []
    for g in range(GROUPS):
        v, m = divmod(g, 4)
        bottom = pltpu.roll(below[v * 8 : v * 8 + 8], (96 - m * 32) % LANES, 1)
        sides.append(jnp.where(lane >= 96, bottom, side_own[g * 8 : g * 8 + 8]))
    x0[SIDE] = jnp.concatenate(sides, axis=0)
    depth_part = jnp.where(lane >= 96, pltpu.roll(below[16:17], 32, 1), depth_side)
    depths.update({STEPS + ROWS + e: below[24 + e : 25 + e] for e in range(4)})
    depths[SIDE] = depth_part
    both_ways(arrive, [], [flux_to_up])
    bottom_flux = fluxes_down[...]
    flux_part = jnp.where(lane >= 96, pltpu.roll(bottom_flux[3:4], 64, 1), flux_side)
    fluxes.update({STEPS + ROWS + e: bottom_flux[e : e + 1] for e in range(3)})
    fluxes[SIDE] = flux_part
    both_ways(arrive, [], rows_out[0::2])
    for step in range(1, STEPS + 1):
        advance(step, list(range(STEPS + step, EXT - step)), False)

    both_ways(arrive, [corner_to_down], [])
    above = from_up[...]
    sides = []
    for g in range(GROUPS):
        v, m = divmod(g, 4)
        top = pltpu.roll(above[v * 8 : v * 8 + 8], (0 - m * 32) % LANES, 1)
        sides.append(jnp.where(lane < 32, top, x0[SIDE, g * 8 : g * 8 + 8]))
    x0[SIDE] = jnp.concatenate(sides, axis=0)
    depths[SIDE] = jnp.where(lane < 32, pltpu.roll(above[16:17], LANES - 64, 1), depth_part)
    depths.update({e: above[28 + e : 29 + e] for e in range(4)})
    both_ways(arrive, [flux_to_down], [])
    top_flux = fluxes_up[...]
    fluxes[SIDE] = jnp.where(lane < 32, pltpu.roll(top_flux[0:1], 64, 1), flux_part)
    fluxes.update({1 + e: top_flux[5 + e : 6 + e] for e in range(3)})
    both_ways(arrive, rows_out[1::2], [])
    for step in range(1, STEPS + 1):
        advance(step, [step, step + 1, step + 2, step + 3], True)
    both_ways(leave, rows_out[0::2], rows_out[1::2])
    for copy in (to_right, to_left, *[regrid(k) for k in range(1, n_lon)]):
        copy.wait_send()

    @pl.when(comp == 0)
    def _():
        regrid(0).wait_send()

    @pl.when(comp == 1)
    def _():
        handed.wait_send()

    both_ways(leave, [corner_to_up, flux_to_up], [corner_to_down, flux_to_down])


def write_rows(rows, out, sem):
    copies = [pltpu.make_async_copy(rows.at[r], out.at[0, :, r, :], sem.at[r]) for r in range(ROWS)]
    for copy in copies:
        copy.start()
    for copy in copies:
        copy.wait()


def on_device(n_lat, n_lon, state, mixing, diffusivity, weights, links, land, depth):
    vmem = pltpu.VMEM
    dma = pltpu.SemaphoreType.DMA
    result = pl.pallas_call(
        functools.partial(kernel, n_lat, n_lon),
        out_shape=pltpu.VMEM((ROWS, LEV, LANES), F32),
        in_specs=[pl.BlockSpec(memory_space=pl.ANY)] * 7,
        out_specs=pl.BlockSpec(memory_space=pltpu.VMEM),
        scratch_shapes=[
            vmem((EXT + 1, LEV, LANES), F32),
            vmem((EXT + 1, LEV, LANES), F32),
            vmem((EXT + 1, LEV, LANES), F32),
            vmem((EXT + 1, LEV, LANES), F32),
            vmem((8, LANES), F32),
            vmem((LEV, LEV), F32),
            vmem(diffusivity.shape, F32),
            vmem(weights.shape, F32),
            vmem((4, LINKS), jnp.int32),
            vmem((1, ROWS), jnp.int32),
            vmem((1, ROWS), jnp.int32),
            vmem((LEV, 3 * LEV + 16), F32),
            vmem((LEV // 2 + 8, LANES), F32),
            vmem((LEV // 2 + 8, LANES), F32),
            vmem((LEV // 2 + 8, LANES), F32),
            vmem((n_lon, 16, LANES), F32),
            vmem((2, n_lon, 16, LANES), F32),
            vmem((32, LANES), F32),
            vmem((32, LANES), F32),
            vmem((32, LANES), F32),
            vmem((32, LANES), F32),
            vmem((8, LANES), F32),
            vmem((8, LANES), F32),
            vmem((8, LANES), F32),
            vmem((8, LANES), F32),
            dma((7 + ROWS,)),
            dma((2 * STEPS,)),
            dma((2 * STEPS,)),
            dma((2,)),
            dma((2,)),
            dma((n_lon,)),
            dma((2, n_lon)),
            dma((2,)),
            dma((2,)),
            dma((2,)),
            dma((2,)),
            vmem((11, LANES), F32),
            vmem((11, LANES), F32),
            dma,
            dma,
        ],
        compiler_params=pltpu.CompilerParams(collective_id=0, has_side_effects=True),
    )(state, mixing, diffusivity, weights, links, land.reshape(1, ROWS), depth.reshape(1, ROWS))
    return pl.pallas_call(
        write_rows,
        out_shape=jax.ShapeDtypeStruct(state.shape, F32),
        in_specs=[pl.BlockSpec(memory_space=pltpu.VMEM)],
        out_specs=pl.BlockSpec(memory_space=pl.ANY),
        scratch_shapes=[dma((ROWS,))],
    )(pltpu.with_memory_space_constraint(result, pltpu.VMEM))


def solution(mesh):
    in_specs = (
        P("comp", None, "lat", "lon"),
        P("comp", None, None),
        P("comp", None),
        P("comp", None),
        P("comp", "lat", "lon", None, None),
        P("lat", "lon"),
        P("lat", "lon"),
    )
    return jax.shard_map(
        functools.partial(on_device, mesh.shape["lat"], mesh.shape["lon"]),
        mesh=mesh,
        in_specs=in_specs,
        out_specs=P("comp", None, "lat", "lon"),
        check_vma=False,
    )
```

```python
import functools

import jax
import jax.numpy as jnp
from jax import lax
from jax.experimental import pallas as pl
from jax.experimental.pallas import tpu as pltpu
from jax.sharding import PartitionSpec as P

MESH = pl.DeviceIdType.MESH
STEPS = 4
LEV = 80
ROWS = 8
LANES = 128
LINKS = 32
GROUPS = LEV // 8
EXT = ROWS + 2 * STEPS
SIDE = EXT
RATE = 0.5
F32 = jnp.float32
BF16 = jnp.bfloat16


def split3(value):
    high = value.astype(BF16)
    rest = value - high.astype(F32)
    middle = rest.astype(BF16)
    low = (rest - middle.astype(F32)).astype(BF16)
    return high, middle, low


def ex0ct_dot(onehot, value):
    return sum(jnp.dot(onehot, part, preferred_element_type=F32) for part in split3(value))


def column(row, size):
    eye = lax.broadcasted_iota(jnp.int32, (size, size), 0) == lax.broadcasted_iota(jnp.int32, (size, size), 1)
    return jnp.sum(jnp.where(eye, jnp.broadcast_to(row, (size, size)), 0.0), axis=1, keepdims=True)


def kernel(
    n_lat,
    n_lon,
    state,
    mixing,
    diffusivity,
    weights,
    links,
    land,
    depth,
    out,
    x0,
    x1,
    x2,
    x3,
    surf,
    mixbuf,
    difbuf,
    wbuf,
    lkbuf,
    landbuf,
    depthbuf,
    mcat,
    pack,
    west,
    east,
    outgoing,
    incoming,
    corner_up,
    corner_down,
    from_up,
    from_down,
    flux_up,
    flux_down,
    fluxes_up,
    fluxes_down,
    load_sem,
    row_send,
    row_recv,
    side_send,
    side_recv,
    regrid_send,
    regrid_recv,
    corner_send,
    corner_recv,
    flux_send,
    flux_recv,
    handing,
    given,
    hand_send,
    hand_recv,
):
    comp, lat, lon = lax.axis_index("comp"), lax.axis_index("lat"), lax.axis_index("lon")
    other = 1 - comp
    up, down = lax.rem(lat + n_lat - 1, n_lat), lax.rem(lat + 1, n_lat)
    left, right = lax.rem(lon + n_lon - 1, n_lon), lax.rem(lon + 1, n_lon)

    has_up, has_down = lat > 0, lat < n_lat - 1
    barrier = pltpu.get_barrier_semaphore()

    def greet(device):
        pl.semaphore_signal(barrier, inc=1, device_id=device, device_id_type=MESH)

    @pl.when(comp == 1)
    def _():
        for k in range(n_lon):
            greet({"comp": 0, "lon": lax.rem(lon + k, n_lon)})
        for k in range(1, n_lon):
            greet({"lon": lax.rem(lon + k, n_lon)})

    @pl.when(comp == 0)
    def _():
        greet({"comp": 1})
        greet({"lon": left})
        greet({"lon": right})

    @pl.when(has_up)
    def _():
        greet({"lat": up})

    @pl.when(has_down)
    def _():
        greet({"lat": down})

    loads = [
        pltpu.make_async_copy(links.at[0, 0, 0], lkbuf, load_sem.at[0]),
        pltpu.make_async_copy(weights, wbuf, load_sem.at[1]),
        pltpu.make_async_copy(state.at[0, 0], surf, load_sem.at[2]),
        pltpu.make_async_copy(land, landbuf, load_sem.at[3]),
        pltpu.make_async_copy(depth, depthbuf, load_sem.at[4]),
        pltpu.make_async_copy(mixing.at[0], mixbuf, load_sem.at[5]),
        pltpu.make_async_copy(diffusivity, difbuf, load_sem.at[6]),
    ]
    for r in range(ROWS):
        loads.append(pltpu.make_async_copy(state.at[0, :, r, :], x0.at[STEPS + r], load_sem.at[7 + r]))
    for load in loads:
        load.start()

    @pl.when(lat == 0)
    def _():
        x0[0:STEPS] = jnp.zeros((STEPS, LEV, LANES), F32)
        from_up[...] = jnp.zeros((32, LANES), F32)
        fluxes_up[...] = jnp.zeros((8, LANES), F32)

    @pl.when(lat == n_lat - 1)
    def _():
        x0[STEPS + ROWS : EXT] = jnp.zeros((STEPS, LEV, LANES), F32)
        from_down[...] = jnp.zeros((32, LANES), F32)
        fluxes_down[...] = jnp.zeros((8, LANES), F32)

    lane = lax.broadcasted_iota(jnp.int32, (1, LANES), 1)
    cell = lane & 7
    low_half = cell < 4
    sub8 = lax.broadcasted_iota(jnp.int32, (8, LANES), 0)
    lane8 = lax.broadcasted_iota(jnp.int32, (8, LANES), 1)

    for load in loads[:3]:
        load.wait()
    table = lkbuf[...].astype(F32)
    source_row, target_row, dest_row, weight_row = (table[i : i + 1, :] for i in range(4))
    source_col, dest_col, weight_col = (column(row, LINKS) for row in (source_row, dest_row, weight_row))
    weight_ids = lax.broadcasted_iota(jnp.int32, (LINKS, wbuf.shape[1]), 1).astype(F32)
    weight = jnp.sum(
        jnp.where(weight_col == weight_ids, jnp.broadcast_to(wbuf[...], weight_ids.shape), 0.0), axis=1, keepdims=True
    )
    surface = surf[...]
    picked = jnp.zeros((LINKS, LANES), F32)
    for b in range(ROWS):
        picked = jnp.where(source_col == float(b), surface[b : b + 1, :], picked)
    row_id = lax.broadcasted_iota(jnp.int32, (n_lon * 8, LINKS), 0)
    place = (row_id.astype(F32) == target_row * 8.0 + dest_row).astype(F32).astype(BF16)
    outgoing[:, 0:8, :] = ex0ct_dot(place, picked * weight).reshape(n_lon, 8, LANES)
    kind = row_id & 7
    dest = row_id >> 3
    before, after = dest - 1, dest + 1
    before = jnp.where(before < 0, n_lon - 1, before)
    after = jnp.where(after >= n_lon, 0, after)
    wanted = jnp.where(kind < 2, before, jnp.where((kind == 4) | (kind == 5), after, dest))
    wanted = jnp.where((kind == 3) | (kind == 7), -1, wanted)
    place_side = (wanted.astype(F32) == target_row).astype(F32).astype(BF16)
    lane32 = lax.broadcasted_iota(jnp.int32, (LINKS, LANES), 1)
    side_row = ((lane32 >> 3) - STEPS).astype(F32)
    side_weight = jnp.where(dest_col == side_row, weight, 0.0)
    ends = jnp.where(lane32 < 8, pltpu.roll(picked, 4, 1), 0.0)
    for shift in (8, 16, 32, 64):
        ends = ends + pltpu.roll(ends, shift, 1)
    both = ex0ct_dot(place_side, jnp.concatenate([side_weight * ends, side_weight], axis=1))
    both = both.reshape(n_lon, 8, 2 * LANES)
    kind3 = lax.broadcasted_iota(jnp.int32, (n_lon, 8, LANES), 1)
    merged = jnp.where((kind3 & 3) == 0, both[:, :, :LANES], both[:, :, LANES:])
    outgoing[:, 8:16, :] = jnp.where(low_half, merged, pltpu.roll(merged, 4, 1))

    loads[3].wait()
    loads[4].wait()
    land_row = landbuf[...].astype(F32)
    depth_row = jnp.where(comp == 1, land_row * depthbuf[...].astype(F32), float(LEV))
    land_col, depth_col = column(land_row, ROWS), column(depth_row, ROWS)
    land_own = jnp.broadcast_to(land_col, (8, LANES))
    depth_own = jnp.broadcast_to(depth_col, (8, LANES))
    mine = (lane8 >> 3) == sub8
    depth_ends = jnp.sum(jnp.where(mine, depth_own, 0.0), axis=0, keepdims=True)
    land_ends = jnp.sum(jnp.where(mine, land_own, 0.0), axis=0, keepdims=True)
    pack[5 * 8 :, :] = jnp.where(sub8 == 0, depth_ends, land_ends)

    for load in loads[7:]:
        load.wait()

    def gather_ends(src, rows, offset):
        total = None
        for e in rows:
            rolled = pltpu.roll(src[e], (e * 8 + 4) % LANES, 1)
            total = rolled if total is None else jnp.where((lane >> 3) == e, rolled, total)
        return total

    own_ends = gather_ends(x0, range(STEPS, STEPS + ROWS), 0)
    lower = pltpu.roll(own_ends[: LEV // 2], LANES - 32, 1)
    upper = pltpu.roll(own_ends[LEV // 2 :], 32, 1)
    pack[: LEV // 2, :] = jnp.where(lane < 64, lower, upper)

    above_here = 1 - lax.div(n_lat - lat, n_lat)
    below_here = 1 - lax.div(lat + 1, n_lat)
    pl.semaphore_wait(barrier, n_lon + 2 * (1 - comp) + above_here + below_here)

    to_right = pltpu.make_async_remote_copy(
        pack, west, side_send.at[0], side_recv.at[0], device_id={"lon": right}, device_id_type=MESH
    )
    to_left = pltpu.make_async_remote_copy(
        pack, east, side_send.at[1], side_recv.at[1], device_id={"lon": left}, device_id_type=MESH
    )
    to_right.start()
    to_left.start()

    def regrid(k):
        d = lax.rem(lon + k, n_lon)
        return pltpu.make_async_remote_copy(
            outgoing.at[d, 0:11],
            incoming.at[comp, lon, 0:11],
            regrid_send.at[k],
            regrid_recv.at[comp, lon],
            device_id={"comp": 1, "lon": d},
            device_id_type=MESH,
        )

    for k in sorted(range(1, n_lon), key=lambda k: -min(k % 8, 8 - k % 8)):
        regrid(k).start()

    @pl.when(comp == 0)
    def _():
        regrid(0).start()

    kept = pltpu.make_async_copy(outgoing.at[lon, 0:11], incoming.at[1, lon, 0:11], regrid_recv.at[1, lon])

    @pl.when(comp == 1)
    def _():
        kept.start()

    rows_out = []
    for ring in range(STEPS):
        rows_out.append(
            pltpu.make_async_remote_copy(
                x0.at[STEPS + ring],
                x0.at[STEPS + ROWS + ring],
                row_send.at[2 * ring],
                row_recv.at[2 * ring],
                device_id={"lat": up},
                device_id_type=MESH,
            )
        )
        rows_out.append(
            pltpu.make_async_remote_copy(
                x0.at[STEPS + ROWS - 1 - ring],
                x0.at[STEPS - 1 - ring],
                row_send.at[2 * ring + 1],
                row_recv.at[2 * ring + 1],
                device_id={"lat": down},
                device_id_type=MESH,
            )
        )

    def both_ways(act, upward, downward):
        @pl.when(has_up)
        def _():
            for copy in upward:
                act(copy)

        @pl.when(has_down)
        def _():
            for copy in downward:
                act(copy)

    start = lambda copy: copy.start()
    arrive = lambda copy: copy.wait_recv()
    leave = lambda copy: copy.wait_send()
    both_ways(start, rows_out[0::2], rows_out[1::2])

    loads[5].wait()
    loads[6].wait()
    mix = mixbuf[...]
    mix_high = mix.astype(BF16).astype(F32)
    mcat[:, 0:LEV] = mix_high
    mcat[:, LEV : 2 * LEV] = mix_high
    mcat[:, 2 * LEV : 3 * LEV] = mix - mix_high
    mcat[:, 3 * LEV :] = jnp.zeros((LEV, 16), F32)
    operator = mcat[...].astype(BF16)
    diffuse = jnp.broadcast_to(column(difbuf[...], LEV), (LEV, LANES))
    level = lax.broadcasted_iota(jnp.int32, (LEV, LANES), 0).astype(F32)

    to_right.wait_recv()
    to_left.wait_recv()
    arrived = jnp.where(low_half, west[...], east[...])
    side_own = jnp.concatenate(
        [pltpu.roll(arrived[: LEV // 2], 32, 1), pltpu.roll(arrived[: LEV // 2], LANES - 32, 1)], axis=0
    )
    masks = pltpu.roll(arrived[LEV // 2 :], 32, 1)
    depth_side, land_side = masks[0:1], masks[1:2]

    def corner(target, base):
        for v in range(3):
            groups = range(v * 4, min(v * 4 + 4, GROUPS))
            total = None
            for m, g in enumerate(groups):
                rolled = pltpu.roll(side_own[g * 8 : g * 8 + 8], (m * 32 - base) % LANES, 1)
                total = rolled if total is None else jnp.where((lane >> 5) == m, rolled, total)
            if v == 2:
                total = jnp.where((lane >> 5) == 2, pltpu.roll(jnp.broadcast_to(depth_side, (8, LANES)), (64 - base) % LANES, 1), total)
            target[v * 8 : v * 8 + 8, :] = total
        target[24:32, :] = depth_own

    corner(corner_up, 32)
    corner(corner_down, 64)
    corner_to_up = pltpu.make_async_remote_copy(
        corner_up, from_down, corner_send.at[0], corner_recv.at[0], device_id={"lat": up}, device_id_type=MESH
    )
    corner_to_down = pltpu.make_async_remote_copy(
        corner_down, from_up, corner_send.at[1], corner_recv.at[1], device_id={"lat": down}, device_id_type=MESH
    )
    both_ways(start, [corner_to_up], [corner_to_down])

    handed = pltpu.make_async_remote_copy(
        handing, given, hand_send, hand_recv, device_id={"comp": 0}, device_id_type=MESH
    )

    def gathered(section):
        for j in range(n_lon):
            copy = pltpu.make_async_remote_copy(
                outgoing.at[j, 0:11],
                incoming.at[section, j, 0:11],
                regrid_send.at[j],
                regrid_recv.at[section, j],
                device_id={"comp": 1, "lon": j},
                device_id_type=MESH,
            )
            copy.wait_recv()
        accum, extra = incoming[section, 0, 0:8, :], incoming[section, 0, 8:11, :]
        for j in range(1, n_lon):
            accum = accum + incoming[section, j, 0:8, :]
            extra = extra + incoming[section, j, 8:11, :]
        return accum, extra

    @pl.when(comp == 1)
    def _():
        accum, extra = gathered(1)
        handing[0:8, :] = accum
        handing[8:11, :] = extra
        handed.start()
        accum, extra = gathered(0)
        given[0:8, :] = accum
        given[8:11, :] = extra

    @pl.when(comp == 0)
    def _():
        handed.wait_recv()

    accum, extra = given[0:8, :], given[8:11, :]
    totals = jnp.sum(
        jnp.where(lane8 == (sub8 + STEPS) * 8, jnp.broadcast_to(extra[2:3], (8, LANES)), 0.0), axis=1, keepdims=True
    )
    flux_own = RATE * land_own * (accum / jnp.maximum(totals, 1.0) - surface)
    flux_side = RATE * land_side * (extra[0:1] / jnp.maximum(extra[1:2], 1.0) - side_own[0:1])
    flux_up[...] = jnp.where(sub8 < 3, flux_own, flux_side)
    flux_down[...] = jnp.where(sub8 >= 5, flux_own, flux_side)
    flux_to_up = pltpu.make_async_remote_copy(
        flux_up, fluxes_down, flux_send.at[0], flux_recv.at[0], device_id={"lat": up}, device_id_type=MESH
    )
    flux_to_down = pltpu.make_async_remote_copy(
        flux_down, fluxes_up, flux_send.at[1], flux_recv.at[1], device_id={"lat": down}, device_id_type=MESH
    )
    both_ways(start, [flux_to_up], [flux_to_down])

    first_lane, last_lane = lane == 0, lane == LANES - 1
    pad = jnp.zeros((16, LANES), BF16)
    levels_at = (x0, x1, x2, x3, out)
    depths = {STEPS + r: depth_own[r : r + 1] for r in range(ROWS)}
    fluxes = {STEPS + r: flux_own[r : r + 1] for r in range(ROWS)}

    def operand(centre, neighbours, e, step):
        moved = centre + diffuse * (neighbours - 4.0 * centre)
        moved = jnp.concatenate([moved[:8] + jnp.where(sub8 == 0, fluxes[e], 0.0), moved[8:]], axis=0)
        active = level < depths[e]
        moved = jnp.where(active, moved, 0.0)
        high = moved.astype(BF16)
        low = (moved - high.astype(F32)).astype(BF16)
        return active, jnp.concatenate([high, low, high, pad], axis=0)

    def side_operand(src, rows, step):
        z = src[SIDE]
        ends = gather_ends(src, rows, 0)
        from_west = pltpu.roll(jnp.where(cell == 3, ends, z), 1, 1)
        from_east = pltpu.roll(jnp.where(cell == 4, ends, z), LANES - 1, 1)
        neighbours = pltpu.roll(z, 8, 1) + pltpu.roll(z, LANES - 8, 1) + from_west + from_east
        return operand(z, neighbours, SIDE, step)

    def row_operand(src, e, step):
        centre = src[e]
        z = pltpu.roll(src[SIDE], (LANES - (e * 8 + 4)) % LANES, 1)
        from_west = pltpu.roll(jnp.where(last_lane, z, centre), 1, 1)
        from_east = pltpu.roll(jnp.where(first_lane, z, centre), LANES - 1, 1)
        return operand(centre, src[e - 1] + src[e + 1] + from_west + from_east, e, step)

    def advance(step, rows, merge):
        src, dst = levels_at[step - 1], levels_at[step]
        tiles = rows + ([SIDE] if step < STEPS else [])
        for at in range(0, len(tiles), 2):
            pair = tiles[at : at + 2]
            parts = [side_operand(src, rows, step) if e == SIDE else row_operand(src, e, step) for e in pair]
            right_side = parts[0][1] if len(pair) == 1 else jnp.concatenate([p[1] for p in parts], axis=1)
            mixed = jnp.dot(operator, right_side, preferred_element_type=F32)
            for i, e in enumerate(pair):
                new = jnp.where(parts[i][0], mixed[:, i * LANES : (i + 1) * LANES], src[e])
                if e == SIDE and merge:
                    new = jnp.where((lane >> 3) <= rows[-1], new, dst[e])
                if step == STEPS:
                    r = e - STEPS
                    dst[r] = new
                else:
                    dst[e] = new

    both_ways(arrive, [], [corner_to_up])
    below = from_down[...]
    sides = []
    for g in range(GROUPS):
        v, m = divmod(g, 4)
        bottom = pltpu.roll(below[v * 8 : v * 8 + 8], (96 - m * 32) % LANES, 1)
        sides.append(jnp.where(lane >= 96, bottom, side_own[g * 8 : g * 8 + 8]))
    x0[SIDE] = jnp.concatenate(sides, axis=0)
    depth_part = jnp.where(lane >= 96, pltpu.roll(below[16:17], 32, 1), depth_side)
    depths.update({STEPS + ROWS + e: below[24 + e : 25 + e] for e in range(4)})
    depths[SIDE] = depth_part
    both_ways(arrive, [], [flux_to_up])
    bottom_flux = fluxes_down[...]
    flux_part = jnp.where(lane >= 96, pltpu.roll(bottom_flux[3:4], 64, 1), flux_side)
    fluxes.update({STEPS + ROWS + e: bottom_flux[e : e + 1] for e in range(3)})
    fluxes[SIDE] = flux_part
    both_ways(arrive, [], rows_out[0::2])
    for step in range(1, STEPS + 1):
        advance(step, list(range(STEPS + step, EXT - step)), False)

    both_ways(arrive, [corner_to_down], [])
    above = from_up[...]
    sides = []
    for g in range(GROUPS):
        v, m = divmod(g, 4)
        top = pltpu.roll(above[v * 8 : v * 8 + 8], (0 - m * 32) % LANES, 1)
        sides.append(jnp.where(lane < 32, top, x0[SIDE, g * 8 : g * 8 + 8]))
    x0[SIDE] = jnp.concatenate(sides, axis=0)
    depths[SIDE] = jnp.where(lane < 32, pltpu.roll(above[16:17], LANES - 64, 1), depth_part)
    depths.update({e: above[28 + e : 29 + e] for e in range(4)})
    both_ways(arrive, [flux_to_down], [])
    top_flux = fluxes_up[...]
    fluxes[SIDE] = jnp.where(lane < 32, pltpu.roll(top_flux[0:1], 64, 1), flux_part)
    fluxes.update({1 + e: top_flux[5 + e : 6 + e] for e in range(3)})
    both_ways(arrive, rows_out[1::2], [])
    for step in range(1, STEPS + 1):
        advance(step, [step, step + 1, step + 2, step + 3], True)
    both_ways(leave, rows_out[0::2], rows_out[1::2])
    for copy in (to_right, to_left, *[regrid(k) for k in range(1, n_lon)]):
        copy.wait_send()

    @pl.when(comp == 0)
    def _():
        regrid(0).wait_send()

    @pl.when(comp == 1)
    def _():
        handed.wait_send()

    both_ways(leave, [corner_to_up, flux_to_up], [corner_to_down, flux_to_down])


def write_rows(rows, out, sem):
    copies = [pltpu.make_async_copy(rows.at[r], out.at[0, :, r, :], sem.at[r]) for r in range(ROWS)]
    for copy in copies:
        copy.start()
    for copy in copies:
        copy.wait()


def on_device(n_lat, n_lon, state, mixing, diffusivity, weights, links, land, depth):
    vmem = pltpu.VMEM
    dma = pltpu.SemaphoreType.DMA
    result = pl.pallas_call(
        functools.partial(kernel, n_lat, n_lon),
        out_shape=pltpu.VMEM((ROWS, LEV, LANES), F32),
        in_specs=[pl.BlockSpec(memory_space=pl.ANY)] * 7,
        out_specs=pl.BlockSpec(memory_space=pltpu.VMEM),
        scratch_shapes=[
            vmem((EXT + 1, LEV, LANES), F32),
            vmem((EXT + 1, LEV, LANES), F32),
            vmem((EXT + 1, LEV, LANES), F32),
            vmem((EXT + 1, LEV, LANES), F32),
            vmem((8, LANES), F32),
            vmem((LEV, LEV), F32),
            vmem(diffusivity.shape, F32),
            vmem(weights.shape, F32),
            vmem((4, LINKS), jnp.int32),
            vmem((1, ROWS), jnp.int32),
            vmem((1, ROWS), jnp.int32),
            vmem((LEV, 3 * LEV + 16), F32),
            vmem((LEV // 2 + 8, LANES), F32),
            vmem((LEV // 2 + 8, LANES), F32),
            vmem((LEV // 2 + 8, LANES), F32),
            vmem((n_lon, 16, LANES), F32),
            vmem((2, n_lon, 16, LANES), F32),
            vmem((32, LANES), F32),
            vmem((32, LANES), F32),
            vmem((32, LANES), F32),
            vmem((32, LANES), F32),
            vmem((8, LANES), F32),
            vmem((8, LANES), F32),
            vmem((8, LANES), F32),
            vmem((8, LANES), F32),
            dma((7 + ROWS,)),
            dma((2 * STEPS,)),
            dma((2 * STEPS,)),
            dma((2,)),
            dma((2,)),
            dma((n_lon,)),
            dma((2, n_lon)),
            dma((2,)),
            dma((2,)),
            dma((2,)),
            dma((2,)),
            vmem((11, LANES), F32),
            vmem((11, LANES), F32),
            dma,
            dma,
        ],
        compiler_params=pltpu.CompilerParams(collective_id=0, has_side_effects=True),
    )(state, mixing, diffusivity, weights, links, land.reshape(1, ROWS), depth.reshape(1, ROWS))
    return pl.pallas_call(
        write_rows,
        out_shape=jax.ShapeDtypeStruct(state.shape, F32),
        in_specs=[pl.BlockSpec(memory_space=pltpu.VMEM)],
        out_specs=pl.BlockSpec(memory_space=pl.ANY),
        scratch_shapes=[dma((ROWS,))],
    )(pltpu.with_memory_space_constraint(result, pltpu.VMEM))


def solution(mesh):
    in_specs = (
        P("comp", None, "lat", "lon"),
        P("comp", None, None),
        P("comp", None),
        P("comp", None),
        P("comp", "lat", "lon", None, None),
        P("lat", "lon"),
        P("lat", "lon"),
    )
    return jax.shard_map(
        functools.partial(on_device, mesh.shape["lat"], mesh.shape["lon"]),
        mesh=mesh,
        in_specs=in_specs,
        out_specs=P("comp", None, "lat", "lon"),
        check_vma=False,
    )
```

```python
import functools

import jax
import jax.numpy as jnp
from jax import lax
from jax.experimental import pallas as pl
from jax.experimental.pallas import tpu as pltpu
from jax.sharding import PartitionSpec as P

MESH = pl.DeviceIdType.MESH
STEPS = 4
LEV = 80
ROWS = 8
LANES = 128
LINKS = 32
GROUPS = LEV // 8
EXT = ROWS + 2 * STEPS
SIDE = EXT
RATE = 0.5
F32 = jnp.float32
BF16 = jnp.bfloat16


def split3(value):
    high = value.astype(BF16)
    rest = value - high.astype(F32)
    middle = rest.astype(BF16)
    low = (rest - middle.astype(F32)).astype(BF16)
    return high, middle, low


def ex0ct_dot(onehot, value):
    return sum(jnp.dot(onehot, part, preferred_element_type=F32) for part in split3(value))


def column(row, size):
    eye = lax.broadcasted_iota(jnp.int32, (size, size), 0) == lax.broadcasted_iota(jnp.int32, (size, size), 1)
    return jnp.sum(jnp.where(eye, jnp.broadcast_to(row, (size, size)), 0.0), axis=1, keepdims=True)


def kernel(
    n_lat,
    n_lon,
    state,
    mixing,
    diffusivity,
    weights,
    links,
    land,
    depth,
    out,
    x0,
    x1,
    x2,
    x3,
    surf,
    mixbuf,
    difbuf,
    wbuf,
    lkbuf,
    landbuf,
    depthbuf,
    mcat,
    pack,
    west,
    east,
    outgoing,
    incoming,
    corner_up,
    corner_down,
    from_up,
    from_down,
    flux_up,
    flux_down,
    fluxes_up,
    fluxes_down,
    load_sem,
    row_send,
    row_recv,
    side_send,
    side_recv,
    regrid_send,
    regrid_recv,
    corner_send,
    corner_recv,
    flux_send,
    flux_recv,
    handing,
    given,
    hand_send,
    hand_recv,
):
    comp, lat, lon = lax.axis_index("comp"), lax.axis_index("lat"), lax.axis_index("lon")
    other = 1 - comp
    up, down = lax.rem(lat + n_lat - 1, n_lat), lax.rem(lat + 1, n_lat)
    left, right = lax.rem(lon + n_lon - 1, n_lon), lax.rem(lon + 1, n_lon)

    has_up, has_down = lat > 0, lat < n_lat - 1
    barrier = pltpu.get_barrier_semaphore()

    def greet(device):
        pl.semaphore_signal(barrier, inc=1, device_id=device, device_id_type=MESH)

    @pl.when(comp == 1)
    def _():
        for k in range(n_lon):
            greet({"comp": 0, "lon": lax.rem(lon + k, n_lon)})
        for k in range(1, n_lon):
            greet({"lon": lax.rem(lon + k, n_lon)})

    @pl.when(comp == 0)
    def _():
        greet({"comp": 1})
        greet({"lon": left})
        greet({"lon": right})

    @pl.when(has_up)
    def _():
        greet({"lat": up})

    @pl.when(has_down)
    def _():
        greet({"lat": down})

    loads = [
        pltpu.make_async_copy(links.at[0, 0, 0], lkbuf, load_sem.at[0]),
        pltpu.make_async_copy(weights, wbuf, load_sem.at[1]),
        pltpu.make_async_copy(state.at[0, 0], surf, load_sem.at[2]),
        pltpu.make_async_copy(land, landbuf, load_sem.at[3]),
        pltpu.make_async_copy(depth, depthbuf, load_sem.at[4]),
        pltpu.make_async_copy(mixing.at[0], mixbuf, load_sem.at[5]),
        pltpu.make_async_copy(diffusivity, difbuf, load_sem.at[6]),
    ]
    for r in range(ROWS):
        loads.append(pltpu.make_async_copy(state.at[0, :, r, :], x0.at[STEPS + r], load_sem.at[7 + r]))
    for load in loads:
        load.start()

    @pl.when(lat == 0)
    def _():
        x0[0:STEPS] = jnp.zeros((STEPS, LEV, LANES), F32)
        from_up[...] = jnp.zeros((32, LANES), F32)
        fluxes_up[...] = jnp.zeros((8, LANES), F32)

    @pl.when(lat == n_lat - 1)
    def _():
        x0[STEPS + ROWS : EXT] = jnp.zeros((STEPS, LEV, LANES), F32)
        from_down[...] = jnp.zeros((32, LANES), F32)
        fluxes_down[...] = jnp.zeros((8, LANES), F32)

    lane = lax.broadcasted_iota(jnp.int32, (1, LANES), 1)
    cell = lane & 7
    low_half = cell < 4
    sub8 = lax.broadcasted_iota(jnp.int32, (8, LANES), 0)
    lane8 = lax.broadcasted_iota(jnp.int32, (8, LANES), 1)

    for load in loads[:3]:
        load.wait()
    table = lkbuf[...].astype(F32)
    source_row, target_row, dest_row, weight_row = (table[i : i + 1, :] for i in range(4))
    source_col, dest_col, weight_col = (column(row, LINKS) for row in (source_row, dest_row, weight_row))
    weight_ids = lax.broadcasted_iota(jnp.int32, (LINKS, wbuf.shape[1]), 1).astype(F32)
    weight = jnp.sum(
        jnp.where(weight_col == weight_ids, jnp.broadcast_to(wbuf[...], weight_ids.shape), 0.0), axis=1, keepdims=True
    )
    surface = surf[...]
    picked = jnp.zeros((LINKS, LANES), F32)
    for b in range(ROWS):
        picked = jnp.where(source_col == float(b), surface[b : b + 1, :], picked)
    row_id = lax.broadcasted_iota(jnp.int32, (n_lon * 8, LINKS), 0)
    place = (row_id.astype(F32) == target_row * 8.0 + dest_row).astype(F32).astype(BF16)
    outgoing[:, 0:8, :] = ex0ct_dot(place, picked * weight).reshape(n_lon, 8, LANES)
    kind = row_id & 7
    dest = row_id >> 3
    before, after = dest - 1, dest + 1
    before = jnp.where(before < 0, n_lon - 1, before)
    after = jnp.where(after >= n_lon, 0, after)
    wanted = jnp.where(kind < 2, before, jnp.where((kind == 4) | (kind == 5), after, dest))
    wanted = jnp.where((kind == 3) | (kind == 7), -1, wanted)
    place_side = (wanted.astype(F32) == target_row).astype(F32).astype(BF16)
    lane32 = lax.broadcasted_iota(jnp.int32, (LINKS, LANES), 1)
    side_row = ((lane32 >> 3) - STEPS).astype(F32)
    side_weight = jnp.where(dest_col == side_row, weight, 0.0)
    ends = jnp.where(lane32 < 8, pltpu.roll(picked, 4, 1), 0.0)
    for shift in (8, 16, 32, 64):
        ends = ends + pltpu.roll(ends, shift, 1)
    both = ex0ct_dot(place_side, jnp.concatenate([side_weight * ends, side_weight], axis=1))
    both = both.reshape(n_lon, 8, 2 * LANES)
    kind3 = lax.broadcasted_iota(jnp.int32, (n_lon, 8, LANES), 1)
    merged = jnp.where((kind3 & 3) == 0, both[:, :, :LANES], both[:, :, LANES:])
    outgoing[:, 8:16, :] = jnp.where(low_half, merged, pltpu.roll(merged, 4, 1))

    loads[3].wait()
    loads[4].wait()
    land_row = landbuf[...].astype(F32)
    depth_row = jnp.where(comp == 1, land_row * depthbuf[...].astype(F32), float(LEV))
    land_col, depth_col = column(land_row, ROWS), column(depth_row, ROWS)
    land_own = jnp.broadcast_to(land_col, (8, LANES))
    depth_own = jnp.broadcast_to(depth_col, (8, LANES))
    mine = (lane8 >> 3) == sub8
    depth_ends = jnp.sum(jnp.where(mine, depth_own, 0.0), axis=0, keepdims=True)
    land_ends = jnp.sum(jnp.where(mine, land_own, 0.0), axis=0, keepdims=True)
    pack[5 * 8 :, :] = jnp.where(sub8 == 0, depth_ends, land_ends)

    for load in loads[7:]:
        load.wait()

    def gather_ends(src, rows, offset):
        total = None
        for e in rows:
            rolled = pltpu.roll(src[e], (e * 8 + 4) % LANES, 1)
            total = rolled if total is None else jnp.where((lane >> 3) == e, rolled, total)
        return total

    own_ends = gather_ends(x0, range(STEPS, STEPS + ROWS), 0)
    lower = pltpu.roll(own_ends[: LEV // 2], LANES - 32, 1)
    upper = pltpu.roll(own_ends[LEV // 2 :], 32, 1)
    pack[: LEV // 2, :] = jnp.where(lane < 64, lower, upper)

    above_here = 1 - lax.div(n_lat - lat, n_lat)
    below_here = 1 - lax.div(lat + 1, n_lat)
    pl.semaphore_wait(barrier, n_lon + 2 * (1 - comp) + above_here + below_here)

    to_right = pltpu.make_async_remote_copy(
        pack, west, side_send.at[0], side_recv.at[0], device_id={"lon": right}, device_id_type=MESH
    )
    to_left = pltpu.make_async_remote_copy(
        pack, east, side_send.at[1], side_recv.at[1], device_id={"lon": left}, device_id_type=MESH
    )
    to_right.start()
    to_left.start()

    def regrid(k):
        d = lax.rem(lon + k, n_lon)
        return pltpu.make_async_remote_copy(
            outgoing.at[d, 0:11],
            incoming.at[comp, lon, 0:11],
            regrid_send.at[k],
            regrid_recv.at[comp, lon],
            device_id={"comp": 1, "lon": d},
            device_id_type=MESH,
        )

    for k in sorted(range(1, n_lon), key=lambda k: -min(k % 8, 8 - k % 8)):
        regrid(k).start()

    @pl.when(comp == 0)
    def _():
        regrid(0).start()

    kept = pltpu.make_async_copy(outgoing.at[lon, 0:11], incoming.at[1, lon, 0:11], regrid_recv.at[1, lon])

    @pl.when(comp == 1)
    def _():
        kept.start()

    rows_out = []
    for ring in range(STEPS):
        rows_out.append(
            pltpu.make_async_remote_copy(
                x0.at[STEPS + ring],
                x0.at[STEPS + ROWS + ring],
                row_send.at[2 * ring],
                row_recv.at[2 * ring],
                device_id={"lat": up},
                device_id_type=MESH,
            )
        )
        rows_out.append(
            pltpu.make_async_remote_copy(
                x0.at[STEPS + ROWS - 1 - ring],
                x0.at[STEPS - 1 - ring],
                row_send.at[2 * ring + 1],
                row_recv.at[2 * ring + 1],
                device_id={"lat": down},
                device_id_type=MESH,
            )
        )

    def both_ways(act, upward, downward):
        @pl.when(has_up)
        def _():
            for copy in upward:
                act(copy)

        @pl.when(has_down)
        def _():
            for copy in downward:
                act(copy)

    start = lambda copy: copy.start()
    arrive = lambda copy: copy.wait_recv()
    leave = lambda copy: copy.wait_send()
    both_ways(start, rows_out[0:6:2], rows_out[1:6:2])

    loads[5].wait()
    loads[6].wait()
    mix = mixbuf[...]
    mix_high = mix.astype(BF16).astype(F32)
    mcat[:, 0:LEV] = mix_high
    mcat[:, LEV : 2 * LEV] = mix_high
    mcat[:, 2 * LEV : 3 * LEV] = mix - mix_high
    mcat[:, 3 * LEV :] = jnp.zeros((LEV, 16), F32)
    operator = mcat[...].astype(BF16)
    diffuse = jnp.broadcast_to(column(difbuf[...], LEV), (LEV, LANES))
    level = lax.broadcasted_iota(jnp.int32, (LEV, LANES), 0).astype(F32)

    to_right.wait_recv()
    to_left.wait_recv()
    arrived = jnp.where(low_half, west[...], east[...])
    side_own = jnp.concatenate(
        [pltpu.roll(arrived[: LEV // 2], 32, 1), pltpu.roll(arrived[: LEV // 2], LANES - 32, 1)], axis=0
    )
    masks = pltpu.roll(arrived[LEV // 2 :], 32, 1)
    depth_side, land_side = masks[0:1], masks[1:2]

    def corner(target, base):
        for v in range(3):
            groups = range(v * 4, min(v * 4 + 4, GROUPS))
            total = None
            for m, g in enumerate(groups):
                rolled = pltpu.roll(side_own[g * 8 : g * 8 + 8], (m * 32 - base) % LANES, 1)
                total = rolled if total is None else jnp.where((lane >> 5) == m, rolled, total)
            if v == 2:
                total = jnp.where((lane >> 5) == 2, pltpu.roll(jnp.broadcast_to(depth_side, (8, LANES)), (64 - base) % LANES, 1), total)
            target[v * 8 : v * 8 + 8, :] = total
        target[24:32, :] = depth_own

    corner(corner_up, 32)
    corner(corner_down, 64)
    corner_to_up = pltpu.make_async_remote_copy(
        corner_up, from_down, corner_send.at[0], corner_recv.at[0], device_id={"lat": up}, device_id_type=MESH
    )
    corner_to_down = pltpu.make_async_remote_copy(
        corner_down, from_up, corner_send.at[1], corner_recv.at[1], device_id={"lat": down}, device_id_type=MESH
    )
    both_ways(start, [corner_to_up, rows_out[6]], [corner_to_down, rows_out[7]])

    handed = pltpu.make_async_remote_copy(
        handing, given, hand_send, hand_recv, device_id={"comp": 0}, device_id_type=MESH
    )

    def gathered(section):
        for j in range(n_lon):
            copy = pltpu.make_async_remote_copy(
                outgoing.at[j, 0:11],
                incoming.at[section, j, 0:11],
                regrid_send.at[j],
                regrid_recv.at[section, j],
                device_id={"comp": 1, "lon": j},
                device_id_type=MESH,
            )
            copy.wait_recv()
        accum, extra = incoming[section, 0, 0:8, :], incoming[section, 0, 8:11, :]
        for j in range(1, n_lon):
            accum = accum + incoming[section, j, 0:8, :]
            extra = extra + incoming[section, j, 8:11, :]
        return accum, extra

    @pl.when(comp == 1)
    def _():
        accum, extra = gathered(1)
        handing[0:8, :] = accum
        handing[8:11, :] = extra
        handed.start()
        accum, extra = gathered(0)
        given[0:8, :] = accum
        given[8:11, :] = extra

    @pl.when(comp == 0)
    def _():
        handed.wait_recv()

    accum, extra = given[0:8, :], given[8:11, :]
    totals = jnp.sum(
        jnp.where(lane8 == (sub8 + STEPS) * 8, jnp.broadcast_to(extra[2:3], (8, LANES)), 0.0), axis=1, keepdims=True
    )
    flux_own = RATE * land_own * (accum / jnp.maximum(totals, 1.0) - surface)
    flux_side = RATE * land_side * (extra[0:1] / jnp.maximum(extra[1:2], 1.0) - side_own[0:1])
    flux_up[...] = jnp.where(sub8 < 3, flux_own, flux_side)
    flux_down[...] = jnp.where(sub8 >= 5, flux_own, flux_side)
    flux_to_up = pltpu.make_async_remote_copy(
        flux_up, fluxes_down, flux_send.at[0], flux_recv.at[0], device_id={"lat": up}, device_id_type=MESH
    )
    flux_to_down = pltpu.make_async_remote_copy(
        flux_down, fluxes_up, flux_send.at[1], flux_recv.at[1], device_id={"lat": down}, device_id_type=MESH
    )
    both_ways(start, [flux_to_up], [flux_to_down])

    first_lane, last_lane = lane == 0, lane == LANES - 1
    pad = jnp.zeros((16, LANES), BF16)
    levels_at = (x0, x1, x2, x3, out)
    depths = {STEPS + r: depth_own[r : r + 1] for r in range(ROWS)}
    fluxes = {STEPS + r: flux_own[r : r + 1] for r in range(ROWS)}

    def operand(centre, neighbours, e, step):
        moved = centre + diffuse * (neighbours - 4.0 * centre)
        moved = jnp.concatenate([moved[:8] + jnp.where(sub8 == 0, fluxes[e], 0.0), moved[8:]], axis=0)
        active = level < depths[e]
        moved = jnp.where(active, moved, 0.0)
        high = moved.astype(BF16)
        low = (moved - high.astype(F32)).astype(BF16)
        return active, jnp.concatenate([high, low, high, pad], axis=0)

    def side_operand(src, rows, step):
        z = src[SIDE]
        ends = gather_ends(src, rows, 0)
        from_west = pltpu.roll(jnp.where(cell == 3, ends, z), 1, 1)
        from_east = pltpu.roll(jnp.where(cell == 4, ends, z), LANES - 1, 1)
        neighbours = pltpu.roll(z, 8, 1) + pltpu.roll(z, LANES - 8, 1) + from_west + from_east
        return operand(z, neighbours, SIDE, step)

    def row_operand(src, e, step):
        centre = src[e]
        z = pltpu.roll(src[SIDE], (LANES - (e * 8 + 4)) % LANES, 1)
        from_west = pltpu.roll(jnp.where(last_lane, z, centre), 1, 1)
        from_east = pltpu.roll(jnp.where(first_lane, z, centre), LANES - 1, 1)
        return operand(centre, src[e - 1] + src[e + 1] + from_west + from_east, e, step)

    def advance(step, rows, merge):
        src, dst = levels_at[step - 1], levels_at[step]
        tiles = rows + ([SIDE] if step < STEPS else [])
        for at in range(0, len(tiles), 2):
            pair = tiles[at : at + 2]
            parts = [side_operand(src, rows, step) if e == SIDE else row_operand(src, e, step) for e in pair]
            right_side = parts[0][1] if len(pair) == 1 else jnp.concatenate([p[1] for p in parts], axis=1)
            mixed = jnp.dot(operator, right_side, preferred_element_type=F32)
            for i, e in enumerate(pair):
                new = jnp.where(parts[i][0], mixed[:, i * LANES : (i + 1) * LANES], src[e])
                if e == SIDE and merge:
                    new = jnp.where((lane >> 3) <= rows[-1], new, dst[e])
                if step == STEPS:
                    r = e - STEPS
                    dst[r] = new
                else:
                    dst[e] = new

    both_ways(arrive, [], [corner_to_up])
    below = from_down[...]
    sides = []
    for g in range(GROUPS):
        v, m = divmod(g, 4)
        bottom = pltpu.roll(below[v * 8 : v * 8 + 8], (96 - m * 32) % LANES, 1)
        sides.append(jnp.where(lane >= 96, bottom, side_own[g * 8 : g * 8 + 8]))
    x0[SIDE] = jnp.concatenate(sides, axis=0)
    depth_part = jnp.where(lane >= 96, pltpu.roll(below[16:17], 32, 1), depth_side)
    depths.update({STEPS + ROWS + e: below[24 + e : 25 + e] for e in range(4)})
    depths[SIDE] = depth_part
    both_ways(arrive, [], [flux_to_up])
    bottom_flux = fluxes_down[...]
    flux_part = jnp.where(lane >= 96, pltpu.roll(bottom_flux[3:4], 64, 1), flux_side)
    fluxes.update({STEPS + ROWS + e: bottom_flux[e : e + 1] for e in range(3)})
    fluxes[SIDE] = flux_part
    both_ways(arrive, [], rows_out[0::2])
    for step in range(1, STEPS + 1):
        advance(step, list(range(STEPS + step, EXT - step)), False)

    both_ways(arrive, [corner_to_down], [])
    above = from_up[...]
    sides = []
    for g in range(GROUPS):
        v, m = divmod(g, 4)
        top = pltpu.roll(above[v * 8 : v * 8 + 8], (0 - m * 32) % LANES, 1)
        sides.append(jnp.where(lane < 32, top, x0[SIDE, g * 8 : g * 8 + 8]))
    x0[SIDE] = jnp.concatenate(sides, axis=0)
    depths[SIDE] = jnp.where(lane < 32, pltpu.roll(above[16:17], LANES - 64, 1), depth_part)
    depths.update({e: above[28 + e : 29 + e] for e in range(4)})
    both_ways(arrive, [flux_to_down], [])
    top_flux = fluxes_up[...]
    fluxes[SIDE] = jnp.where(lane < 32, pltpu.roll(top_flux[0:1], 64, 1), flux_part)
    fluxes.update({1 + e: top_flux[5 + e : 6 + e] for e in range(3)})
    both_ways(arrive, rows_out[1::2], [])
    for step in range(1, STEPS + 1):
        advance(step, [step, step + 1, step + 2, step + 3], True)
    both_ways(leave, rows_out[0::2], rows_out[1::2])
    for copy in (to_right, to_left, *[regrid(k) for k in range(1, n_lon)]):
        copy.wait_send()

    @pl.when(comp == 0)
    def _():
        regrid(0).wait_send()

    @pl.when(comp == 1)
    def _():
        handed.wait_send()

    both_ways(leave, [corner_to_up, flux_to_up], [corner_to_down, flux_to_down])


def write_rows(rows, out, sem):
    copies = [pltpu.make_async_copy(rows.at[r], out.at[0, :, r, :], sem.at[r]) for r in range(ROWS)]
    for copy in copies:
        copy.start()
    for copy in copies:
        copy.wait()


def on_device(n_lat, n_lon, state, mixing, diffusivity, weights, links, land, depth):
    vmem = pltpu.VMEM
    dma = pltpu.SemaphoreType.DMA
    result = pl.pallas_call(
        functools.partial(kernel, n_lat, n_lon),
        out_shape=pltpu.VMEM((ROWS, LEV, LANES), F32),
        in_specs=[pl.BlockSpec(memory_space=pl.ANY)] * 7,
        out_specs=pl.BlockSpec(memory_space=pltpu.VMEM),
        scratch_shapes=[
            vmem((EXT + 1, LEV, LANES), F32),
            vmem((EXT + 1, LEV, LANES), F32),
            vmem((EXT + 1, LEV, LANES), F32),
            vmem((EXT + 1, LEV, LANES), F32),
            vmem((8, LANES), F32),
            vmem((LEV, LEV), F32),
            vmem(diffusivity.shape, F32),
            vmem(weights.shape, F32),
            vmem((4, LINKS), jnp.int32),
            vmem((1, ROWS), jnp.int32),
            vmem((1, ROWS), jnp.int32),
            vmem((LEV, 3 * LEV + 16), F32),
            vmem((LEV // 2 + 8, LANES), F32),
            vmem((LEV // 2 + 8, LANES), F32),
            vmem((LEV // 2 + 8, LANES), F32),
            vmem((n_lon, 16, LANES), F32),
            vmem((2, n_lon, 16, LANES), F32),
            vmem((32, LANES), F32),
            vmem((32, LANES), F32),
            vmem((32, LANES), F32),
            vmem((32, LANES), F32),
            vmem((8, LANES), F32),
            vmem((8, LANES), F32),
            vmem((8, LANES), F32),
            vmem((8, LANES), F32),
            dma((7 + ROWS,)),
            dma((2 * STEPS,)),
            dma((2 * STEPS,)),
            dma((2,)),
            dma((2,)),
            dma((n_lon,)),
            dma((2, n_lon)),
            dma((2,)),
            dma((2,)),
            dma((2,)),
            dma((2,)),
            vmem((11, LANES), F32),
            vmem((11, LANES), F32),
            dma,
            dma,
        ],
        compiler_params=pltpu.CompilerParams(collective_id=0, has_side_effects=True),
    )(state, mixing, diffusivity, weights, links, land.reshape(1, ROWS), depth.reshape(1, ROWS))
    return pl.pallas_call(
        write_rows,
        out_shape=jax.ShapeDtypeStruct(state.shape, F32),
        in_specs=[pl.BlockSpec(memory_space=pltpu.VMEM)],
        out_specs=pl.BlockSpec(memory_space=pl.ANY),
        scratch_shapes=[dma((ROWS,))],
    )(pltpu.with_memory_space_constraint(result, pltpu.VMEM))


def solution(mesh):
    in_specs = (
        P("comp", None, "lat", "lon"),
        P("comp", None, None),
        P("comp", None),
        P("comp", None),
        P("comp", "lat", "lon", None, None),
        P("lat", "lon"),
        P("lat", "lon"),
    )
    return jax.shard_map(
        functools.partial(on_device, mesh.shape["lat"], mesh.shape["lon"]),
        mesh=mesh,
        in_specs=in_specs,
        out_specs=P("comp", None, "lat", "lon"),
        check_vma=False,
    )
```
